32 devices in a mesh: dp: 4 (over x, core), vocab: 8 (over z, y).
Axes of the slice: x: 2, y: 2, z: 4, core: 2. Of those that a mesh axis runs over, the one named last changes fastest.
Arguments:
- token_ids: int32 [32, 512], P(('dp', 'vocab')), may hold values from 0 to 30719, as said below
- lengths: int32 [32], P(('dp', 'vocab')), may hold values from 1 to 512, as said below
- word_table: bfloat16 [30720, 768], P('vocab'), may hold values from -6 to 6
- position_table: bfloat16 [512, 768], P('vocab'), may hold values from -3 to 3
- embed_gain: bfloat16 [768], P('vocab'), may hold values from 0.5 to 1.5
- embed_bias: bfloat16 [768], P('vocab'), may hold values from -3 to 3
- query_weight: bfloat16 [768, 768], P('vocab'), may hold values from -0.21875 to 0.21875
- query_bias: bfloat16 [768], P('vocab'), may hold values from -3 to 3
- key_weight: bfloat16 [768, 768], P('vocab'), may hold values from -0.21875 to 0.21875
- value_weight: bfloat16 [768, 768], P('vocab'), may hold values from -0.21875 to 0.21875
- value_bias: bfloat16 [768], P('vocab'), may hold values from -3 to 3
- output_weight: bfloat16 [768, 768], P('vocab'), may hold values from -0.875 to 0.875
- output_bias: bfloat16 [768], P('vocab'), may hold values from -3 to 3
- middle_gain: bfloat16 [768], P('vocab'), may hold values from 0.5 to 1.5
- middle_bias: bfloat16 [768], P('vocab'), may hold values from -3 to 3
- inner_weight: bfloat16 [768, 3072], P('vocab'), may hold values from -0.21875 to 0.21875
- inner_bias: bfloat16 [3072], P('vocab'), may hold values from -3 to 3
- outer_weight: bfloat16 [3072, 768], P('vocab'), may hold values from -0.109375 to 0.109375
- outer_bias: bfloat16 [768], P('vocab'), may hold values from -3 to 3
- final_gain: bfloat16 [768], P('vocab'), may hold values from 0.5 to 1.5
- final_bias: bfloat16 [768], P('vocab'), may hold values from -3 to 3
- cotangent: bfloat16 [32, 512, 768], P(('dp', 'vocab')), may hold values from -6 to 6
Outputs:
- activations: bfloat16 [32, 512, 768], P(('dp', 'vocab'))
- table_gradient: float32 [30720, 768], P('vocab')
- position_gradient: float32 [512, 768], P('vocab')
- embed_gain_gradient: float32 [768], P('vocab')
- embed_bias_gradient: float32 [768], P('vocab')
- query_weight_gradient: float32 [768, 768], P('vocab')
- query_bias_gradient: float32 [768], P('vocab')
- key_weight_gradient: float32 [768, 768], P('vocab')
- value_weight_gradient: float32 [768, 768], P('vocab')
- value_bias_gradient: float32 [768], P('vocab')
- output_weight_gradient: float32 [768, 768], P('vocab')
- output_bias_gradient: float32 [768], P('vocab')
- middle_gain_gradient: float32 [768], P('vocab')
- middle_bias_gradient: float32 [768], P('vocab')
- inner_weight_gradient: float32 [768, 3072], P('vocab')
- inner_bias_gradient: float32 [3072], P('vocab')
- outer_weight_gradient: float32 [3072, 768], P('vocab')
- outer_bias_gradient: float32 [768], P('vocab')
- final_gain_gradient: float32 [768], P('vocab')
- final_bias_gradient: float32 [768], P('vocab')
The draws below stay inside these ranges and needn't reach their ends.
Inputs may be any that keep to these rules, and one draw needn't show every extreme that they name: Passage p holds real tokens in its first lengths[p] slots, the rest are padding that no query attends to; some passage is full. `token_ids`: the table's rows fall into equal blocks, one for each index of vocab; of the 512 slots of one device, at most 128 hold ids of one block, and on every device exactly 128 slots hold ids of some block.
All inputs are finite; a program needn't handle non-finite values.
Results may differ from the reference program's by a relative error of at most 0.02.
Values may be sent and summed in bfloat16 or wider, within the bound.
No kernel may reach another device: no remote copies, remote signals or barrier semaphores. Data moves between devices by JAX's collectives and lax.ppermute only.
A program may use at most 192 MiB of HBM per device.

```python
import math
import jax
import jax.numpy as jnp
from jax import lax

D = 768
HEADS = 12
FF = 3072
LEN = 512
VOCAB = 30720
SEQ_DEV = 1
TOK_DEV = 512
PASSAGES = 32
CAP = 128
N_VOCAB = 8


def draw_lengths(key, part):
    key_one, key_two, key_three, key_four = jax.random.split(key, 4)
    shorter = jnp.minimum(jax.random.randint(key_one, (PASSAGES,), 1, LEN + 1), jax.random.randint(key_two, (PASSAGES,), 1, LEN + 1))
    lifted = jnp.maximum(shorter, jax.random.randint(key_three, (PASSAGES,), 1, LEN + 1))
    chosen = jax.random.randint(key_four, (), 0, PASSAGES)
    return jnp.where(lax.iota(jnp.int32, PASSAGES) == chosen, LEN, lifted).astype(jnp.int32)


def device_ids(key):
    keys = jax.random.split(key, 7)
    owners = N_VOCAB
    block_rows = VOCAB // N_VOCAB
    heavy = jax.random.randint(keys[0], (), 0, owners)
    first = jax.random.randint(keys[1], (TOK_DEV,), 0, owners)
    second = jax.random.randint(keys[2], (TOK_DEV,), 0, owners)
    pick_heavy = jax.random.randint(keys[3], (TOK_DEV,), 0, 4) == 0
    owner = jnp.where(pick_heavy, heavy, (jnp.minimum(first, second) + heavy) % owners)
    owner = jnp.where(lax.iota(jnp.int32, TOK_DEV) < CAP, heavy, owner).astype(jnp.int32)
    onehot = (owner[:, None] == lax.iota(jnp.int32, owners)[None, :]).astype(jnp.int32)
    rank = jnp.sum((jnp.cumsum(onehot, axis=0) - 1) * onehot, axis=1)
    kept = rank < CAP
    load = jnp.minimum(jnp.sum(onehot, axis=0), CAP)
    room = jnp.cumsum(CAP - load)
    spill = jnp.cumsum(jnp.where(kept, 0, 1)) - 1
    moved = jnp.sum((room[None, :] <= spill[:, None]).astype(jnp.int32), axis=1)
    owner = jnp.where(kept, owner, moved).astype(jnp.int32)
    owner = owner[jax.random.permutation(keys[4], TOK_DEV)]
    left = jax.random.randint(keys[5], (TOK_DEV,), 0, block_rows)
    right = jax.random.randint(keys[6], (TOK_DEV,), 0, block_rows)
    local = left * right // block_rows
    return (owner * block_rows + local).astype(jnp.int32)


def draw_token_ids(key, part):
    devices_all = PASSAGES // SEQ_DEV
    keys = jax.random.split(key, devices_all)
    ids = jax.vmap(device_ids)(keys)
    return ids.reshape(PASSAGES, LEN).astype(jnp.int32)


def with_spikes(entries, own_key, source, target, blocks, factor):
    owner, partner = [(jnp.arange(entries.shape[dim]) // (entries.shape[dim] // blocks)).reshape([-1 if axis == dim else 1 for axis in range(entries.ndim)]) for dim in (source, target)]
    chosen = jax.random.permutation(own_key, blocks)[partner]
    strong = (owner == chosen) | (owner == (partner + blocks // 2) % blocks)
    return jnp.where(strong, factor * entries, entries)


def levels(stream_key, shape, pieces, smallest, top_value):
    factor_of, own = 1.0, jax.random.fold_in(stream_key, 6)
    for dim, blocks in pieces:
        draws = jnp.exp(jax.random.uniform(jax.random.fold_in(own, dim), (blocks,), jnp.float32, smallest / len(pieces), top_value / len(pieces)))
        factor_of = factor_of * jnp.repeat(draws, shape[dim] // blocks).reshape([-1 if axis == dim else 1 for axis in range(len(shape))])
    return factor_of


def gaussian(stream_key, dims, scale, most, cuts=(), held_as=jnp.bfloat16):
    loudness = levels(stream_key, dims, cuts, -0.22, 0.18) if cuts else 1.0
    values = jax.random.normal(stream_key, dims, jnp.float32) * scale * loudness
    return jnp.minimum(jnp.maximum(values, -most), most).astype(held_as)


def heavy_noise(rng, extent, scale, bound, cuts, heavy, kind=jnp.bfloat16):
    entries = scale * jax.random.normal(rng, extent, jnp.float32)
    if cuts:
        entries = entries * levels(rng, extent, cuts, -0.22, 0.18)
    return jnp.clip(with_spikes(entries, jax.random.fold_in(rng, 3), *heavy), -bound, bound).astype(kind)


def setup_inputs(seed: int = 0) -> dict:
    seeds = jax.random.split(jax.random.key(seed), 23)
    return {
        "token_ids": draw_token_ids(jax.random.fold_in(seeds[22], 71), 0),
        "lengths": draw_lengths(jax.random.fold_in(seeds[22], 71), 0),
        "word_table": gaussian(seeds[2], (VOCAB, D), 1.0, 6.0, ((0, 8),)),
        "position_table": gaussian(seeds[3], (LEN, D), 0.5, 3.0, ((0, 8),)),
        "embed_gain": jnp.clip(1.0 + 0.1 * jax.random.normal(seeds[4], (D,), jnp.float32), 0.5, 1.5).astype(jnp.bfloat16),
        "embed_bias": gaussian(seeds[5], (D,), 0.5, 3.0, ((0, 8),)),
        "query_weight": gaussian(seeds[6], (D, D), D ** -0.5, 0.21875, ((0, 8),)),
        "query_bias": gaussian(seeds[7], (D,), 0.5, 3.0, ((0, 8),)),
        "key_weight": gaussian(seeds[8], (D, D), D ** -0.5, 0.21875, ((0, 8),)),
        "value_weight": gaussian(seeds[9], (D, D), D ** -0.5, 0.21875, ((0, 8),)),
        "value_bias": gaussian(seeds[10], (D,), 0.5, 3.0, ((0, 8),)),
        "output_weight": gaussian(seeds[11], (D, D), (D // 16) ** -0.5, 0.875, ((0, 8),)),
        "output_bias": gaussian(seeds[12], (D,), 0.5, 3.0, ((0, 8),)),
        "middle_gain": jnp.clip(1.0 + 0.1 * jax.random.normal(seeds[13], (D,), jnp.float32), 0.5, 1.5).astype(jnp.bfloat16),
        "middle_bias": gaussian(seeds[14], (D,), 0.5, 3.0, ((0, 8),)),
        "inner_weight": gaussian(seeds[15], (D, FF), D ** -0.5, 0.21875, ((0, 8),)),
        "inner_bias": gaussian(seeds[16], (FF,), 0.5, 3.0, ((0, 8),)),
        "outer_weight": gaussian(seeds[17], (FF, D), FF ** -0.5, 0.109375, ((0, 8),)),
        "outer_bias": gaussian(seeds[18], (D,), 0.5, 3.0, ((0, 8),)),
        "final_gain": jnp.clip(1.0 + 0.1 * jax.random.normal(seeds[19], (D,), jnp.float32), 0.5, 1.5).astype(jnp.bfloat16),
        "final_bias": gaussian(seeds[20], (D,), 0.5, 3.0, ((0, 8),)),
        "cotangent": heavy_noise(seeds[21], (PASSAGES, LEN, D), 1.0, 6.0, ((0, 32),), (0, 2, 32, 2.75)),
    }


@jax.custom_vjp
def low(v):
    return lax.optimization_barrier(v.astype(jnp.bfloat16)).astype(jnp.float32)

@jax.custom_vjp
def low_back(v):
    return v

def low_keep(v):
    return (low(v), None)

def low_pass(kept, grad):
    return (grad,)

def back_keep(v):
    return (v, None)

def back_low(kept, grad):
    return (low(grad),)
low.defvjp(low_keep, low_pass)
low_back.defvjp(back_keep, back_low)

def layer_norm(values, gain, bias_row):
    center = values - lax.optimization_barrier(jnp.mean(values, axis=-1, keepdims=True))
    variance = lax.optimization_barrier(jnp.mean(center * center, axis=-1, keepdims=True))
    return center * lax.rsqrt(variance + 1e-12) * gain + bias_row

def dense(left, right):
    return jnp.einsum('gtd,de->gte', left, right, precision=lax.Precision.HIGHEST)

def block_rows(params, id_group, length_group):
    table, position, embed_scale, embed_shift, query_matrix, query_shift, key_matrix, value_matrix, value_shift, output_matrix, output_shift, middle_scale, middle_shift, inner_matrix, inner_shift, outer_matrix, outer_shift, final_scale, final_shift = params
    passages_here = id_group.shape[0]
    embedded = low_back(jnp.take(table, id_group, axis=0))
    normed = layer_norm(embedded + position[None], embed_scale, embed_shift)
    normed_low = low(normed)
    queries = low_back(low(dense(normed_low, query_matrix) + query_shift))
    key_rows = low_back(low(dense(normed_low, key_matrix)))
    value_rows = low_back(low(dense(normed_low, value_matrix) + value_shift))
    head_dim = D // HEADS
    query_heads = queries.reshape(passages_here, LEN, HEADS, head_dim)
    key_heads = key_rows.reshape(passages_here, LEN, HEADS, head_dim)
    value_heads = value_rows.reshape(passages_here, LEN, HEADS, head_dim)
    scores = jnp.einsum('gqhd,gkhd->ghqk', query_heads, key_heads, precision=lax.Precision.HIGHEST) * 0.125
    scores = low_back(scores)
    visible = lax.iota(jnp.int32, LEN)[None, :] < length_group[:, None].astype(jnp.int32)
    scores = jnp.where(visible[:, None, None, :], scores, -1e+30)
    probs = low(jax.nn.softmax(scores, axis=-1))
    context = jnp.einsum('ghqk,gkhd->gqhd', probs, value_heads, precision=lax.Precision.HIGHEST)
    context = low_back(low(context.reshape(passages_here, LEN, D)))
    attended = low_back(dense(context, output_matrix) + output_shift)
    middle = layer_norm(normed + attended, middle_scale, middle_shift)
    middle_low = low(middle)
    inner = low_back(dense(middle_low, inner_matrix) + inner_shift)
    activated = low(jax.nn.gelu(inner, approximate=False))
    branch = low_back(dense(activated, outer_matrix) + outer_shift)
    return layer_norm(middle + branch, final_scale, final_shift)

def reference(token_ids, lengths, word_table, position_table, embed_gain, embed_bias, query_weight, query_bias, key_weight, value_weight, value_bias, output_weight, output_bias, middle_gain, middle_bias, inner_weight, inner_bias, outer_weight, outer_bias, final_gain, final_bias, cotangent):
    params = tuple((item.astype(jnp.float32) for item in (word_table, position_table, embed_gain, embed_bias, query_weight, query_bias, key_weight, value_weight, value_bias, output_weight, output_bias, middle_gain, middle_bias, inner_weight, inner_bias, outer_weight, outer_bias, final_gain, final_bias)))
    group = math.gcd(PASSAGES, 8)
    blocks = PASSAGES // group
    id_blocks = token_ids.reshape(blocks, group, LEN)
    length_blocks = lengths.reshape(blocks, group)
    upstream = cotangent.astype(jnp.float32).reshape(blocks, group, LEN, D)

    def forward(weights):

        def one_group(inputs):
            return block_rows(weights, inputs[0], inputs[1])
        return lax.map(jax.checkpoint(one_group), (id_blocks, length_blocks))
    result, pullback = jax.vjp(forward, params)
    gradients = pullback(upstream)[0]
    output = result.reshape(PASSAGES, LEN, D)
    return (output.astype(jnp.bfloat16), gradients[0], gradients[1], gradients[2], gradients[3], gradients[4], gradients[5], gradients[6], gradients[7], gradients[8], gradients[9], gradients[10], gradients[11], gradients[12], gradients[13], gradients[14], gradients[15], gradients[16], gradients[17], gradients[18])
```

```python
import functools
import math

import jax
import jax.numpy as jnp
from jax import lax
from jax.sharding import PartitionSpec as P

HEADS = 12


epsilon = 1e-12
scaling = 0.125


def normalize(values, gain, bias_row):
    center = values - jnp.mean(values, axis=-1, keepdims=True)
    inverse = lax.rsqrt(jnp.mean(center * center, axis=-1, keepdims=True) + epsilon)
    scaled = center * inverse
    return (scaled * gain + bias_row, scaled, inverse)


def normalize_back(upstream, scaled, inverse, gain):
    weighted = upstream * gain
    return inverse * (
        weighted
        - jnp.mean(weighted, axis=-1, keepdims=True)
        - scaled * jnp.mean(weighted * scaled, axis=-1, keepdims=True)
    )


def gelu_slope(inner):
    cumulative = 0.5 * (1.0 + lax.erf(inner * (1.0 / math.sqrt(2.0))))
    density = jnp.exp(-0.5 * inner * inner) * (1.0 / math.sqrt(2.0 * math.pi))
    return cumulative + inner * density


def matmul(left, right):
    return jnp.dot(left, right, preferred_element_type=jnp.float32)


def contract_rows(left, right):
    return jnp.einsum("ti,tj->ij", left, right, preferred_element_type=jnp.float32)


def times_transposed(left, right):
    return jnp.einsum("tj,ij->ti", left, right, preferred_element_type=jnp.float32)


def split_heads(rows):
    return rows.reshape(rows.shape[0], HEADS, rows.shape[1] // HEADS)


def masked_scores(query_heads, key_heads, visible):
    scores = (
        jnp.einsum("qhd,khd->hqk", query_heads, key_heads, preferred_element_type=jnp.float32)
        * scaling
    )
    return jnp.where(visible[None, None, :], scores, -1e30)


def attend(inputs):
    query_rows, key_rows, value_rows, visible = inputs
    query_heads = split_heads(query_rows)
    scores = masked_scores(query_heads, split_heads(key_rows), visible)
    largest = jnp.max(scores, axis=-1, keepdims=True)
    raised = jnp.exp(scores - largest)
    totals = jnp.sum(raised, axis=-1, keepdims=True)
    probs = raised / totals
    context = jnp.einsum(
        "hqk,khd->qhd",
        probs.astype(jnp.bfloat16),
        split_heads(value_rows),
        preferred_element_type=jnp.float32,
    )
    return (context.reshape(query_rows.shape).astype(jnp.bfloat16), largest + jnp.log(totals))


def attend_back(inputs):
    query_rows, key_rows, value_rows, visible, kept_lse, context_grad = inputs
    query_heads = split_heads(query_rows)
    key_heads = split_heads(key_rows)
    value_heads = split_heads(value_rows)
    grad_heads = split_heads(context_grad)
    probs = jnp.exp(masked_scores(query_heads, key_heads, visible) - kept_lse)
    prob_grad = jnp.einsum(
        "qhd,khd->hqk", grad_heads, value_heads, preferred_element_type=jnp.float32
    )
    centered = prob_grad - jnp.sum(prob_grad * probs, axis=-1, keepdims=True)
    score_grad = (probs * centered).astype(jnp.bfloat16)
    query_grad = (
        jnp.einsum("hqk,khd->qhd", score_grad, key_heads, preferred_element_type=jnp.float32)
        * scaling
    )
    key_grad = (
        jnp.einsum("hqk,qhd->khd", score_grad, query_heads, preferred_element_type=jnp.float32)
        * scaling
    )
    value_grad = jnp.einsum(
        "hqk,qhd->khd", probs.astype(jnp.bfloat16), grad_heads, preferred_element_type=jnp.float32
    )
    return (
        query_grad.reshape(query_rows.shape),
        key_grad.reshape(key_rows.shape),
        value_grad.reshape(value_rows.shape),
    )


class Links:
    def __init__(self, groups, owners):
        self.groups, self.owners = groups, owners
        self.A = 4 if owners % 4 == 0 else 1
        self.B = owners // self.A
        A, B = self.A, self.B
        self.ring_a = [(a * B + b, (a + 1) % A * B + b) for a in range(A) for b in range(B)]
        self.ring_b = [(a * B + b, a * B + (b + 1) % B) for a in range(A) for b in range(B)]

    def place(self):
        vocab = lax.axis_index("vocab")
        return vocab // self.B, vocab % self.B

    def step_a(self, piece):
        return lax.ppermute(piece, "vocab", self.ring_a)

    def step_b(self, piece):
        return lax.ppermute(piece, "vocab", self.ring_b)

    def swap(self, piece, bit):
        return lax.ppermute(piece, "dp", [(i, i ^ bit) for i in range(self.groups)])

    def spread(self, piece, axis=0):
        a, b = self.place()
        shape = piece.shape[:axis] + (self.owners,) + piece.shape[axis:]
        out = jnp.zeros(shape, piece.dtype)
        held = piece
        for k in range(self.A):
            if k:
                held = self.step_a(held)
            row = held
            for m in range(self.B):
                if m:
                    row = self.step_b(row)
                where = (a - k) % self.A * self.B + (b - m) % self.B
                out = lax.dynamic_update_index_in_dim(out, row, where, axis)
        return out

    def fold(self, total, axis=0):
        a, b = self.place()
        shape = total.shape[:axis] + (self.A, self.B) + total.shape[axis + 1 :]
        total = total.reshape(shape)

        def ring(whole, count, here, step, axis):
            def block(index):
                return lax.dynamic_index_in_dim(whole, index % count, axis, keepdims=False)

            held = block(here - 1 + count)
            for s in range(1, count):
                held = add(step(held), block(here - 1 - s + 2 * count))
            return held

        total = ring(total, self.B, b, self.step_b, axis + 1)
        return ring(total, self.A, a, self.step_a, axis)

    def far(self, piece, first):
        bit = first
        while bit < self.groups:
            piece = add(piece, self.swap(piece, bit))
            bit *= 2
        return piece


def add(left, right):
    return (left.astype(jnp.float32) + right.astype(jnp.float32)).astype(jnp.bfloat16)


def gelu(inner):
    return inner * (0.5 * (1.0 + lax.erf(inner * (1.0 / math.sqrt(2.0)))))


def put(blocks, where, axis):
    shape = blocks[0].shape[:axis] + (len(blocks),) + blocks[0].shape[axis:]
    out = jnp.zeros(shape, blocks[0].dtype)
    for block, index in zip(blocks, where):
        out = lax.dynamic_update_index_in_dim(out, block, index, axis)
    return out


def pick(stacked, index, axis=0):
    return lax.dynamic_index_in_dim(stacked, index, axis, keepdims=False)


def on_device(
    groups,
    owners,
    token_ids,
    lengths,
    word_table,
    position_table,
    embed_gain,
    embed_bias,
    query_weight,
    query_bias,
    key_weight,
    value_weight,
    value_bias,
    output_weight,
    output_bias,
    middle_gain,
    middle_bias,
    inner_weight,
    inner_bias,
    outer_weight,
    outer_bias,
    final_gain,
    final_bias,
    cotangent,
):
    links = Links(groups, owners)
    table_rows, width = word_table.shape
    full_len = token_ids.shape[1]
    piece_rows = query_weight.shape[0]
    hidden = inner_weight.shape[1]
    cap = 2 * full_len // owners
    dp = lax.axis_index("dp")
    core, quarter = dp % 2, dp % 4
    ids = token_ids.reshape(full_len)

    owner = ids // table_rows
    local = ids - owner * table_rows
    onehot = owner[:, None] == lax.iota(jnp.int32, owners)[None, :]
    before = lax.iota(jnp.int32, full_len)
    lower = (before[:, None] > before[None, :]).astype(jnp.bfloat16)
    ranks = matmul(lower, onehot.astype(jnp.bfloat16))
    rank = jnp.sum(jnp.where(onehot, ranks, 0.0), axis=1).astype(jnp.int32)
    slot = owner * cap + rank
    slots = lax.iota(jnp.int32, owners * cap)
    sent_ids = jnp.sum(
        jnp.where(slots[:, None] == slot[None, :], local[None, :] + 1, 0), axis=1
    ) - 1
    held_ids = lax.all_to_all(sent_ids.reshape(owners, cap), "vocab", 0, 0, tiled=True).reshape(-1)
    picked = jnp.take(word_table, jnp.maximum(held_ids, 0), axis=0)
    arrived = lax.all_to_all(picked.reshape(owners, cap, width), "vocab", 0, 0, tiled=True)
    route = (slot[:, None] == slots[None, :]).astype(jnp.bfloat16)
    embedded = matmul(route, arrived.reshape(owners * cap, width))

    vectors = [
        embed_gain, embed_bias, query_bias, value_bias, output_bias, middle_gain, middle_bias,
        outer_bias, final_gain, final_bias,
    ]
    small = jnp.concatenate(vectors + [inner_bias])
    small_rows = -(-small.shape[0] // width)
    small = jnp.pad(small, (0, small_rows * width - small.shape[0])).reshape(small_rows, width)
    place_part = position_table.shape[0] // 2
    place_half = lax.dynamic_slice_in_dim(position_table, core * place_part, place_part, 0)
    first_message = links.spread(jnp.concatenate([place_half, small]))
    place_here = first_message[:, :place_part]
    place_there = links.swap(place_here, 1)
    place_rows = put([place_here, place_there], [core, 1 - core], 1).reshape(full_len, width)
    small = first_message[:, place_part:].reshape(owners, small_rows * width)
    vector = [
        small[:, i * piece_rows : (i + 1) * piece_rows].reshape(width).astype(jnp.float32)
        for i in range(len(vectors))
    ]
    (
        embed_scale, embed_shift, query_shift, value_shift, output_shift, middle_scale,
        middle_shift, outer_shift, final_scale, final_shift,
    ) = vector
    inner_shift = (
        small[:, len(vectors) * piece_rows :][:, : inner_bias.shape[0]]
        .reshape(hidden)
        .astype(jnp.float32)
    )

    square = jnp.stack([query_weight, key_weight, value_weight, output_weight])
    pair_here = links.spread(lax.dynamic_slice_in_dim(square, 2 * core, 2, 0), 1)
    pair_there = links.swap(pair_here, 1)
    four = put([pair_here, pair_there], [core, 1 - core], 0).reshape(4, width, width)
    query_matrix, key_matrix, value_matrix, output_matrix = (four[i] for i in range(4))

    blocks = [quarter, quarter ^ 1, quarter ^ 2, quarter ^ 3]

    def quad(piece):
        beside = links.swap(piece, 1)
        beyond = links.swap(piece, 2)
        return [piece, beside, beyond, links.swap(beyond, 1)]

    inner_part = links.spread(lax.dynamic_slice_in_dim(inner_weight, quarter * width, width, 1))
    inner_matrix = put(quad(inner_part.reshape(width, width)), blocks, 0)
    outer_part = links.spread(
        lax.dynamic_slice_in_dim(outer_weight, quarter * piece_rows, piece_rows, 0)
    )
    outer_matrix = put(quad(outer_part), blocks, 1).reshape(hidden, width)

    summed = embedded + place_rows.astype(jnp.float32)
    normed, hat_embed, inv_embed = normalize(summed, embed_scale, embed_shift)
    normed_low = normed.astype(jnp.bfloat16)
    query_low = (matmul(normed_low, query_matrix) + query_shift).astype(jnp.bfloat16)
    key_low = matmul(normed_low, key_matrix).astype(jnp.bfloat16)
    value_low = (matmul(normed_low, value_matrix) + value_shift).astype(jnp.bfloat16)
    visible = lax.iota(jnp.int32, full_len) < lengths[0]
    context, lse_kept = attend((query_low, key_low, value_low, visible))
    attended = matmul(context, output_matrix) + output_shift
    middle, hat_middle, inv_middle = normalize(normed + attended, middle_scale, middle_shift)
    middle_low = middle.astype(jnp.bfloat16)
    inner = (
        jnp.concatenate([matmul(middle_low, inner_matrix[i]) for i in range(4)], axis=1)
        + inner_shift
    )
    activated = gelu(inner).astype(jnp.bfloat16)
    branch = matmul(activated, outer_matrix) + outer_shift
    result, hat_final, inv_final = normalize(middle + branch, final_scale, final_shift)
    output = result.astype(jnp.bfloat16).reshape(1, full_len, width)

    upstream = cotangent.reshape(full_len, width).astype(jnp.float32)
    final_gain_gradient = jnp.sum(upstream * hat_final, axis=0)
    final_bias_gradient = jnp.sum(upstream, axis=0)
    second = normalize_back(upstream, hat_final, inv_final, final_scale)
    branch_grad = second.astype(jnp.bfloat16)
    outer_bias_gradient = jnp.sum(branch_grad.astype(jnp.float32), axis=0)

    def shared(parts):
        beside = links.swap(jnp.stack([parts[1], parts[3]]), 1)
        near, across = add(parts[0], beside[0]), add(parts[2], beside[1])
        whole = add(near, links.swap(across, 2))
        return links.far(links.fold(whole), 4)

    outer_grad = contract_rows(activated, branch_grad).astype(jnp.bfloat16)
    outer_grad = outer_grad.reshape(owners, 4, piece_rows, width)
    outer_share = shared([pick(outer_grad, i, 1) for i in blocks])
    inner_grad = (times_transposed(branch_grad, outer_matrix) * gelu_slope(inner)).astype(
        jnp.bfloat16
    )
    inner_bias_gradient = jnp.sum(inner_grad.astype(jnp.float32), axis=0)
    inner_parts = [inner_grad[:, i * width : (i + 1) * width] for i in range(4)]
    inner_grads = jnp.stack(
        [contract_rows(middle_low, part).astype(jnp.bfloat16) for part in inner_parts]
    ).reshape(4, owners, piece_rows, width)
    inner_share = shared([pick(inner_grads, i) for i in blocks])
    middle_grad = second + sum(
        times_transposed(inner_parts[i], inner_matrix[i]) for i in range(4)
    )
    middle_gain_gradient = jnp.sum(middle_grad * hat_middle, axis=0)
    middle_bias_gradient = jnp.sum(middle_grad, axis=0)
    first = normalize_back(middle_grad, hat_middle, inv_middle, middle_scale)
    attended_grad = first.astype(jnp.bfloat16)
    output_bias_gradient = jnp.sum(attended_grad.astype(jnp.float32), axis=0)
    output_grad = contract_rows(context, attended_grad).astype(jnp.bfloat16)
    context_grad = times_transposed(attended_grad, output_matrix).astype(jnp.bfloat16)
    query_grad, key_grad, value_grad = attend_back(
        (query_low, key_low, value_low, visible, lse_kept, context_grad)
    )
    query_low_grad = query_grad.astype(jnp.bfloat16)
    key_low_grad = key_grad.astype(jnp.bfloat16)
    value_low_grad = value_grad.astype(jnp.bfloat16)
    query_bias_gradient = jnp.sum(query_low_grad.astype(jnp.float32), axis=0)
    value_bias_gradient = jnp.sum(value_low_grad.astype(jnp.float32), axis=0)
    normed_grad = (
        first
        + times_transposed(query_low_grad, query_matrix)
        + times_transposed(key_low_grad, key_matrix)
        + times_transposed(value_low_grad, value_matrix)
    )
    embed_gain_gradient = jnp.sum(normed_grad * hat_embed, axis=0)
    embed_bias_gradient = jnp.sum(normed_grad, axis=0)
    summed_grad = normalize_back(normed_grad, hat_embed, inv_embed, embed_scale)
    embedded_grad = summed_grad.astype(jnp.bfloat16)

    leaving = jnp.einsum(
        "ts,td->sd", route, embedded_grad, preferred_element_type=jnp.float32
    ).astype(jnp.bfloat16)
    landed = lax.all_to_all(leaving.reshape(owners, cap, width), "vocab", 0, 0, tiled=True)
    landed = landed.reshape(1, owners * cap, width)
    known = held_ids[None]
    bit = 1
    while bit < groups:
        low_side = (dp // bit) % 2 == 0

        def joined(own, bit=bit, low_side=low_side):
            other = links.swap(own, bit)
            return jnp.concatenate(
                [jnp.where(low_side, own, other), jnp.where(low_side, other, own)]
            )

        landed, known = joined(landed), joined(known)
        bit *= 2
    landed, known = landed.reshape(-1, width), known.reshape(-1)
    half_rows = table_rows // 2
    half_ids = core * half_rows + lax.iota(jnp.int32, half_rows)
    table_half = matmul(
        (half_ids[:, None] == known[None, :]).astype(jnp.bfloat16), landed
    ).astype(jnp.bfloat16)
    table_other = links.swap(table_half, 1)
    table_gradient = jnp.concatenate(
        [
            jnp.where(core == 0, table_half, table_other).astype(jnp.float32),
            jnp.where(core == 0, table_other, table_half).astype(jnp.float32),
        ]
    )

    square_grads = jnp.stack(
        [
            contract_rows(normed_low, query_low_grad).astype(jnp.bfloat16),
            contract_rows(normed_low, key_low_grad).astype(jnp.bfloat16),
            contract_rows(normed_low, value_low_grad).astype(jnp.bfloat16),
            output_grad,
        ]
    ).reshape(2, 2, owners, piece_rows, width)
    mine = add(pick(square_grads, core), links.swap(pick(square_grads, 1 - core), 1))
    pair_share = links.far(links.fold(mine, 1), 2)
    pair_other = links.swap(pair_share, 1)
    four_shares = put([pair_share, pair_other], [core, 1 - core], 0)
    four_shares = four_shares.reshape(4, piece_rows, width).astype(jnp.float32)

    place_grads = summed_grad.astype(jnp.bfloat16).reshape(owners, 2, place_part, width)
    place_mine = add(
        pick(place_grads, core, 1), links.swap(pick(place_grads, 1 - core, 1), 1)
    )
    place_share = links.far(links.fold(place_mine), 2)
    place_other = links.swap(place_share, 1)
    position_gradient = put([place_share, place_other], [core, 1 - core], 0)
    position_gradient = position_gradient.reshape(2 * place_part, width).astype(jnp.float32)

    def regroup(share, axis):
        return put(quad(share), blocks, axis).astype(jnp.float32)

    inner_weight_gradient = regroup(inner_share, 1).reshape(piece_rows, hidden)
    outer_weight_gradient = regroup(outer_share, 0).reshape(4 * piece_rows, width)

    sums = [
        embed_gain_gradient, embed_bias_gradient, query_bias_gradient, value_bias_gradient,
        output_bias_gradient, middle_gain_gradient, middle_bias_gradient, outer_bias_gradient,
        final_gain_gradient, final_bias_gradient,
    ]
    table = jnp.concatenate(
        [item.reshape(owners, piece_rows) for item in sums]
        + [inner_bias_gradient.reshape(owners, inner_bias.shape[0])],
        axis=1,
    ).astype(jnp.bfloat16)
    vector_share = links.far(links.fold(table), 1).astype(jnp.float32)
    pieces = [vector_share[i * piece_rows : (i + 1) * piece_rows] for i in range(len(sums))]
    inner_bias_gradient = vector_share[len(sums) * piece_rows :]
    (
        embed_gain_gradient, embed_bias_gradient, query_bias_gradient, value_bias_gradient,
        output_bias_gradient, middle_gain_gradient, middle_bias_gradient, outer_bias_gradient,
        final_gain_gradient, final_bias_gradient,
    ) = pieces
    return (
        output,
        table_gradient,
        position_gradient,
        embed_gain_gradient,
        embed_bias_gradient,
        four_shares[0],
        query_bias_gradient,
        four_shares[1],
        four_shares[2],
        value_bias_gradient,
        four_shares[3],
        output_bias_gradient,
        middle_gain_gradient,
        middle_bias_gradient,
        inner_weight_gradient,
        inner_bias_gradient,
        outer_weight_gradient,
        outer_bias_gradient,
        final_gain_gradient,
        final_bias_gradient,
    )


def solution(mesh):
    return jax.shard_map(
        functools.partial(on_device, mesh.shape["dp"], mesh.shape["vocab"]),
        mesh=mesh,
        in_specs=(
            P(("dp", "vocab"), None),
            P(("dp", "vocab")),
            P("vocab", None),
            P("vocab", None),
            P("vocab"),
            P("vocab"),
            P("vocab", None),
            P("vocab"),
            P("vocab", None),
            P("vocab", None),
            P("vocab"),
            P("vocab", None),
            P("vocab"),
            P("vocab"),
            P("vocab"),
            P("vocab", None),
            P("vocab"),
            P("vocab", None),
            P("vocab"),
            P("vocab"),
            P("vocab"),
            P(("dp", "vocab"), None, None),
        ),
        out_specs=(
            P(("dp", "vocab"), None, None),
            P("vocab", None),
            P("vocab", None),
            P("vocab"),
            P("vocab"),
            P("vocab", None),
            P("vocab"),
            P("vocab", None),
            P("vocab", None),
            P("vocab"),
            P("vocab", None),
            P("vocab"),
            P("vocab"),
            P("vocab"),
            P("vocab", None),
            P("vocab"),
            P("vocab", None),
            P("vocab"),
            P("vocab"),
            P("vocab"),
        ),
        check_vma=False,
    )
```

```python
import functools
import math

import jax
import jax.numpy as jnp
from jax import lax
from jax.experimental import pallas as pl
from jax.experimental.pallas import tpu as pltpu
from jax.sharding import PartitionSpec as P

HEADS = 12


epsilon = 1e-12
scaling = 0.125


def normalize(values, gain, bias_row):
    center = values - jnp.mean(values, axis=-1, keepdims=True)
    inverse = lax.rsqrt(jnp.mean(center * center, axis=-1, keepdims=True) + epsilon)
    scaled = center * inverse
    return (scaled * gain + bias_row, scaled, inverse)


def normalize_back(upstream, scaled, inverse, gain):
    weighted = upstream * gain
    return inverse * (
        weighted
        - jnp.mean(weighted, axis=-1, keepdims=True)
        - scaled * jnp.mean(weighted * scaled, axis=-1, keepdims=True)
    )


def gelu_slope(inner):
    cumulative = 0.5 * (1.0 + lax.erf(inner * (1.0 / math.sqrt(2.0))))
    density = jnp.exp(-0.5 * inner * inner) * (1.0 / math.sqrt(2.0 * math.pi))
    return cumulative + inner * density


def matmul(left, right):
    return jnp.dot(left, right, preferred_element_type=jnp.float32)


def contract_rows(left, right):
    return jnp.einsum("ti,tj->ij", left, right, preferred_element_type=jnp.float32)


def times_transposed(left, right):
    return jnp.einsum("tj,ij->ti", left, right, preferred_element_type=jnp.float32)


def split_heads(rows):
    return rows.reshape(rows.shape[0], HEADS, rows.shape[1] // HEADS)


def masked_scores(query_heads, key_heads, visible):
    scores = (
        jnp.einsum("qhd,khd->hqk", query_heads, key_heads, preferred_element_type=jnp.float32)
        * scaling
    )
    return jnp.where(visible[None, None, :], scores, -1e30)


def attend(inputs):
    query_rows, key_rows, value_rows, visible = inputs
    query_heads = split_heads(query_rows)
    scores = masked_scores(query_heads, split_heads(key_rows), visible)
    largest = jnp.max(scores, axis=-1, keepdims=True)
    raised = jnp.exp(scores - largest)
    totals = jnp.sum(raised, axis=-1, keepdims=True)
    probs = raised / totals
    context = jnp.einsum(
        "hqk,khd->qhd",
        probs.astype(jnp.bfloat16),
        split_heads(value_rows),
        preferred_element_type=jnp.float32,
    )
    return (context.reshape(query_rows.shape).astype(jnp.bfloat16), largest + jnp.log(totals))


def attend_back(inputs):
    query_rows, key_rows, value_rows, visible, kept_lse, context_grad = inputs
    query_heads = split_heads(query_rows)
    key_heads = split_heads(key_rows)
    value_heads = split_heads(value_rows)
    grad_heads = split_heads(context_grad)
    probs = jnp.exp(masked_scores(query_heads, key_heads, visible) - kept_lse)
    prob_grad = jnp.einsum(
        "qhd,khd->hqk", grad_heads, value_heads, preferred_element_type=jnp.float32
    )
    centered = prob_grad - jnp.sum(prob_grad * probs, axis=-1, keepdims=True)
    score_grad = (probs * centered).astype(jnp.bfloat16)
    query_grad = (
        jnp.einsum("hqk,khd->qhd", score_grad, key_heads, preferred_element_type=jnp.float32)
        * scaling
    )
    key_grad = (
        jnp.einsum("hqk,qhd->khd", score_grad, query_heads, preferred_element_type=jnp.float32)
        * scaling
    )
    value_grad = jnp.einsum(
        "hqk,qhd->khd", probs.astype(jnp.bfloat16), grad_heads, preferred_element_type=jnp.float32
    )
    return (
        query_grad.reshape(query_rows.shape),
        key_grad.reshape(key_rows.shape),
        value_grad.reshape(value_rows.shape),
    )


class Links:
    def __init__(self, groups, owners):
        self.groups, self.owners = groups, owners
        self.A = 4 if owners % 4 == 0 else 1
        self.B = owners // self.A

    def place(self):
        vocab = lax.axis_index("vocab")
        return vocab // self.B, vocab % self.B

    def step_a(self, piece, far=1):
        A, B = self.A, self.B
        pairs = [(a * B + b, (a + far) % A * B + b) for a in range(A) for b in range(B)]
        return lax.ppermute(piece, "vocab", pairs)

    def step_b(self, piece):
        A, B = self.A, self.B
        pairs = [(a * B + b, a * B + (b + 1) % B) for a in range(A) for b in range(B)]
        return lax.ppermute(piece, "vocab", pairs)

    def swap(self, piece, bit):
        return lax.ppermute(piece, "dp", [(i, i ^ bit) for i in range(self.groups)])

    def row(self, piece):
        pieces = [piece]
        for _ in range(1, self.B):
            pieces.append(self.step_b(pieces[-1]))
        return pieces

    def sources(self):
        a, b = self.place()
        A, B = self.A, self.B
        return jnp.stack([(a - k + A) % A * B + (b - m + B) % B for k in range(A) for m in range(B)])

    def fold_b(self, total, axis):
        B = self.B
        here = self.place()[1]

        def block(index):
            return pick(total, index % B, axis + 1)

        held = block(here - 1 + B)
        for s in range(1, B):
            held = add(self.step_b(held), block(here - 1 - s + 2 * B))
        return held

    def fold_a(self, total, axis):
        A = self.A
        here = self.place()[0]
        terms = [pick(total, here, axis)]
        for far in range(1, A):
            terms.append(self.step_a(pick(total, (here + far) % A, axis), far))
        return add(*terms)

    def split(self, total, axis):
        return total.reshape(total.shape[:axis] + (self.A, self.B) + total.shape[axis + 1 :])

    def far(self, piece, first):
        bit = first
        while bit < self.groups:
            piece = add(piece, self.swap(piece, bit))
            bit *= 2
        return piece


def add(*terms):
    return sum(term.astype(jnp.float32) for term in terms).astype(jnp.bfloat16)


def tie(*values):
    return lax.optimization_barrier(values)


def gelu(inner):
    return inner * (0.5 * (1.0 + lax.erf(inner * (1.0 / math.sqrt(2.0)))))


def pick(stacked, index, axis=0):
    return lax.dynamic_index_in_dim(stacked, index, axis, keepdims=False)


def arrange(sources, pieces, bands, lanes):
    owners = len(pieces)

    def body(sources_ref, *refs):
        ins, outs = refs[:owners], refs[owners:]
        for i in range(owners):
            where = sources_ref[i]
            for (start, size), wide, out in zip(bands, lanes, outs):
                out[where] = ins[i][start : start + size, :wide]

    return pl.pallas_call(
        body,
        out_shape=tuple(
            jax.ShapeDtypeStruct((owners, size, wide), pieces[0].dtype)
            for (start, size), wide in zip(bands, lanes)
        ),
        in_specs=[pl.BlockSpec(memory_space=pltpu.SMEM)]
        + [pl.BlockSpec(memory_space=pltpu.VMEM)] * owners,
        out_specs=tuple(pl.BlockSpec(memory_space=pltpu.VMEM) for _ in bands),
        cost_estimate=pl.CostEstimate(
            flops=0, bytes_accessed=4 * owners * pieces[0].size, transcendentals=0
        ),
        name="arrange",
    )(sources, *pieces)


def cost(micros):
    return pl.CostEstimate(flops=0, bytes_accessed=int(micros * 3e6), transcendentals=0)


def whole(count):
    return [pl.BlockSpec(memory_space=pltpu.VMEM)] * count


SMEM = pl.BlockSpec(memory_space=pltpu.SMEM)


def dot(left, right, dims=((1,), (0,))):
    return lax.dot_general(left, right, (dims, ((), ())), preferred_element_type=jnp.float32)


def head_masks(shape):
    low = lax.broadcasted_iota(jnp.int32, shape, 1) < shape[1] // 2
    return low, jnp.logical_not(low)


def attend_kernel(length_ref, query_ref, key_ref, value_ref, context_ref):
    count, wide = query_ref.shape[0], 2 * query_ref.shape[1] // HEADS
    hidden_keys = lax.broadcasted_iota(jnp.int32, (count, count), 1) >= length_ref[0]

    @pl.loop(0, HEADS // 2)
    def _(pair):
        lanes = pl.ds(pl.multiple_of(pair * wide, wide), wide)
        query, key, value = query_ref[:, lanes], key_ref[:, lanes], value_ref[:, lanes]
        query = query * scaling
        masks = head_masks((count, wide))
        parts = []
        for mask in masks:
            scores = dot(jnp.where(mask, query, 0).astype(jnp.bfloat16), key, ((1,), (1,)))
            scores = jnp.where(hidden_keys, -1e30, scores)
            raised = jnp.exp(scores - jnp.max(scores, axis=1, keepdims=True))
            totals = jnp.sum(raised, axis=1, keepdims=True)
            parts.append(dot(raised.astype(jnp.bfloat16), value) / totals)
        context_ref[:, lanes] = jnp.where(masks[0], parts[0], parts[1]).astype(jnp.bfloat16)


def attend_call(length, query, key, value):
    return pl.pallas_call(
        attend_kernel,
        out_shape=jax.ShapeDtypeStruct(query.shape, jnp.bfloat16),
        in_specs=[SMEM] + whole(3),
        out_specs=pl.BlockSpec(memory_space=pltpu.VMEM),
        cost_estimate=cost(4),
        name="attend",
    )(length, query, key, value)


def attend_back_kernel(
    length_ref, query_ref, key_ref, value_ref, grad_ref,
    query_grad_ref, key_grad_ref, value_grad_ref, query_sum_ref, value_sum_ref,
):
    count, wide = query_ref.shape[0], 2 * query_ref.shape[1] // HEADS
    half = wide // 2
    hidden_keys = lax.broadcasted_iota(jnp.int32, (count, count), 0) >= length_ref[0]

    @pl.loop(0, HEADS // 2)
    def _(pair):
        lanes = pl.ds(pl.multiple_of(pair * wide, wide), wide)
        query, key = query_ref[:, lanes] * scaling, key_ref[:, lanes]
        query = query.astype(jnp.bfloat16)
        value, grad = value_ref[:, lanes], grad_ref[:, lanes]
        across = jnp.transpose(key.astype(jnp.float32)).astype(jnp.bfloat16)
        masks = head_masks((count, wide))
        query_parts, key_parts, value_parts = [], [], []
        for i, mask in enumerate(masks):
            scores = dot(key, jnp.where(mask, query, 0).astype(jnp.bfloat16), ((1,), (1,)))
            scores = jnp.where(hidden_keys, -1e30, scores)
            raised = jnp.exp(scores - jnp.max(scores, axis=0, keepdims=True))
            probs = raised * (1.0 / jnp.sum(raised, axis=0, keepdims=True))
            prob_grad = dot(jnp.where(mask, value, 0).astype(jnp.bfloat16), grad, ((1,), (1,)))
            centered = prob_grad - jnp.sum(prob_grad * probs, axis=0, keepdims=True)
            score_grad = (probs * centered).astype(jnp.bfloat16)
            value_parts.append(dot(probs.astype(jnp.bfloat16), grad))
            key_parts.append(dot(score_grad, query))
            query_parts.append(dot(across[i * half : (i + 1) * half], score_grad))
        value_grad = jnp.where(masks[0], value_parts[0], value_parts[1]).astype(jnp.bfloat16)
        value_grad_ref[:, lanes] = value_grad
        value_sum_ref[:, lanes] = jnp.sum(value_grad.astype(jnp.float32), axis=0, keepdims=True)
        key_grad = jnp.where(masks[0], key_parts[0], key_parts[1])
        key_grad_ref[:, lanes] = key_grad.astype(jnp.bfloat16)
        query_grad = jnp.transpose(jnp.concatenate(query_parts, axis=0) * scaling)
        query_grad = query_grad.astype(jnp.bfloat16)
        query_grad_ref[:, lanes] = query_grad
        query_sum_ref[:, lanes] = jnp.sum(query_grad.astype(jnp.float32), axis=0, keepdims=True)


def attend_back_call(length, query, key, value, grad):
    like = jax.ShapeDtypeStruct(query.shape, jnp.bfloat16)
    line = jax.ShapeDtypeStruct((1, query.shape[1]), jnp.float32)
    return pl.pallas_call(
        attend_back_kernel,
        out_shape=(like, like, like, line, line),
        in_specs=[SMEM] + whole(4),
        out_specs=tuple(whole(5)),
        cost_estimate=cost(3),
        name="attend_back",
    )(length, query, key, value, grad)


def hidden_kernel(rows_ref, shift_ref, *refs):
    inner_refs, outer_refs, active_refs, slope_refs = (refs[4 * i : 4 * i + 4] for i in range(4))
    branch_ref = refs[16]
    width = rows_ref.shape[1]
    tile = 256
    branch_ref[...] = jnp.zeros_like(branch_ref)
    for i in range(4):

        @pl.loop(0, width // tile)
        def _(part, i=i):
            lanes = pl.ds(pl.multiple_of(part * tile, tile), tile)
            inner = dot(rows_ref[...], inner_refs[i][:, lanes]) + shift_ref[i : i + 1, lanes]
            cumulative = 0.5 * (1.0 + lax.erf(inner * (1.0 / math.sqrt(2.0))))
            density = jnp.exp(-0.5 * inner * inner) * (1.0 / math.sqrt(2.0 * math.pi))
            active = (inner * cumulative).astype(jnp.bfloat16)
            active_refs[i][:, lanes] = active
            slope_refs[i][:, lanes] = (cumulative + inner * density).astype(jnp.bfloat16)
            branch_ref[...] += dot(active, outer_refs[i][lanes, :])


def hidden_call(rows, shift, inner, outer):
    like = jax.ShapeDtypeStruct(rows.shape, jnp.bfloat16)
    out = pl.pallas_call(
        hidden_kernel,
        out_shape=(like,) * 8 + (jax.ShapeDtypeStruct(rows.shape, jnp.float32),),
        in_specs=whole(10),
        out_specs=tuple(whole(9)),
        cost_estimate=cost(8),
        name="hidden",
    )(rows, shift, *inner, *outer)
    return out[:4], out[4:8], out[8]


def widen_kernel(core_ref, here_ref, there_ref, out_ref):
    wide = here_ref.shape[1]

    @pl.when(core_ref[0] == 0)
    def _():
        out_ref[:, :wide] = here_ref[...].astype(jnp.float32)
        out_ref[:, wide:] = there_ref[...].astype(jnp.float32)

    @pl.when(core_ref[0] != 0)
    def _():
        out_ref[:, :wide] = there_ref[...].astype(jnp.float32)
        out_ref[:, wide:] = here_ref[...].astype(jnp.float32)


def widen_call(core, here, there):
    count, wide = here.shape
    tile = count // 8
    return pl.pallas_call(
        widen_kernel,
        grid=(8,),
        out_shape=jax.ShapeDtypeStruct((count, 2 * wide), jnp.float32),
        in_specs=[SMEM] + [pl.BlockSpec((tile, wide), lambda i: (i, 0))] * 2,
        out_specs=pl.BlockSpec((tile, 2 * wide), lambda i: (i, 0)),
        cost_estimate=cost(5),
        name="widen",
    )(core.reshape(1), here, there)


def on_device(
    groups,
    owners,
    token_ids,
    lengths,
    word_table,
    position_table,
    embed_gain,
    embed_bias,
    query_weight,
    query_bias,
    key_weight,
    value_weight,
    value_bias,
    output_weight,
    output_bias,
    middle_gain,
    middle_bias,
    inner_weight,
    inner_bias,
    outer_weight,
    outer_bias,
    final_gain,
    final_bias,
    cotangent,
):
    links = Links(groups, owners)
    table_rows, width = word_table.shape
    full_len = token_ids.shape[1]
    rows = query_weight.shape[0]
    hidden = inner_weight.shape[1]
    cap = 2 * full_len // owners
    place_part = position_table.shape[0] // 2
    dp = lax.axis_index("dp")
    core, quarter = dp % 2, dp % 4
    blocks = [quarter, quarter ^ 1, quarter ^ 2, quarter ^ 3]
    ids = token_ids.reshape(full_len)

    inner_quarter = pick(inner_weight.reshape(rows, owners, 4, rows), quarter, 2)
    hidden_piece = jnp.concatenate(
        [
            inner_quarter.reshape(rows, width),
            lax.dynamic_slice_in_dim(outer_weight, quarter * rows, rows, 0),
        ]
    )
    vectors = [
        embed_gain, embed_bias, query_bias, value_bias, output_bias, middle_gain, middle_bias,
        outer_bias, final_gain, final_bias,
    ]
    vectors += [inner_bias[i * rows : (i + 1) * rows] for i in range(4)]
    vector_piece = sum(
        lax.pad(
            item.reshape(1, rows),
            jnp.zeros((), jnp.bfloat16),
            ((i, 15 - i, 0), (0, width - rows, 0)),
        )
        for i, item in enumerate(vectors)
    )
    square_piece = jnp.concatenate(
        [
            jnp.where(core == 0, query_weight, value_weight),
            jnp.where(core == 0, key_weight, output_weight),
            lax.dynamic_slice_in_dim(position_table, core * place_part, place_part, 0),
            vector_piece,
        ]
    )

    owner = ids // table_rows
    local = ids - owner * table_rows
    onehot = owner[:, None] == lax.iota(jnp.int32, owners)[None, :]
    before = lax.iota(jnp.int32, full_len)
    lower = (before[:, None] > before[None, :]).astype(jnp.bfloat16)
    ranks = matmul(lower, onehot.astype(jnp.bfloat16))
    rank = jnp.sum(jnp.where(onehot, ranks, 0.0), axis=1).astype(jnp.int32)
    slot = owner * cap + rank
    slots = lax.iota(jnp.int32, owners * cap)
    sent_ids = jnp.sum(
        jnp.where(slots[:, None] == slot[None, :], local[None, :] + 1, 0), axis=1
    ) - 1
    held_ids = lax.all_to_all(sent_ids.reshape(owners, cap), "vocab", 0, 0, tiled=True).reshape(-1)

    picked = jnp.take(word_table, jnp.maximum(held_ids, 0), axis=0)
    hidden_pieces, square_pieces, beyond_pieces = [], [], []
    hidden_held, square_held = hidden_piece, square_piece
    A = links.A
    plan = [(0, 0, None), (1, None, 0), (2, 1, None), (3, 2, 1)]
    if A == 1:
        plan = [(0, None, None)]
    arrived = None
    for square_step, hidden_step, cross in plan:
        square_row = links.row(square_held)
        square_next = links.step_a(square_held) if square_step < A - 1 else ()
        hidden_row, hidden_next, crossing = (), (), ()
        if hidden_step is not None:
            hidden_row, hidden_next = links.row(hidden_held), links.step_a(hidden_held)
        if cross is not None:
            here = slice(cross * links.B, (cross + 1) * links.B)
            crossing = [links.swap(piece, 2) for piece in hidden_pieces[here]]
        tied = tie(square_row, square_next, hidden_row, hidden_next, crossing, picked)
        square_row, square_next, hidden_row, hidden_next, crossing, picked = tied
        square_pieces += square_row
        hidden_pieces += hidden_row
        beyond_pieces += crossing
        square_held = square_next
        if hidden_step is not None:
            hidden_held = hidden_next
        if arrived is None:
            arrived = lax.all_to_all(
                picked.reshape(owners, cap, width), "vocab", 0, 0, tiled=True
            )
    sources = links.sources()
    first_here, second_here, place_here, small = arrange(
        sources,
        square_pieces,
        [(0, rows), (rows, rows), (2 * rows, place_part), (2 * rows + place_part, 16)],
        [width, width, width, 128 * -(-rows // 128)],
    )
    first_there, second_there, place_there = (
        links.swap(item, 1) for item in (first_here, second_here, place_here)
    )
    hidden_row = links.row(hidden_held)
    first_cross = [links.swap(p, 2) for p in hidden_pieces[len(beyond_pieces) :]]

    small = jnp.transpose(small[:, :, :rows], (1, 0, 2)).reshape(16, width).astype(jnp.float32)
    (
        embed_scale, embed_shift, query_shift, value_shift, output_shift, middle_scale,
        middle_shift, outer_shift, final_scale, final_shift,
    ) = (small[i] for i in range(10))
    inner_shift = jnp.stack([pick(small, 10 + i) for i in blocks])

    def ordered(here, there):
        return jnp.where(core == 0, here, there), jnp.where(core == 0, there, here)

    query_matrix, value_matrix = ordered(
        first_here.reshape(width, width), first_there.reshape(width, width)
    )
    key_matrix, output_matrix = ordered(
        second_here.reshape(width, width), second_there.reshape(width, width)
    )
    place_rows = jnp.stack(ordered(place_here, place_there), axis=1).reshape(full_len, width)

    route = (slot[:, None] == slots[None, :]).astype(jnp.bfloat16)
    embedded = matmul(route, arrived.reshape(owners * cap, width))
    summed = embedded + place_rows.astype(jnp.float32)
    normed, hat_embed, inv_embed = normalize(summed, embed_scale, embed_shift)
    normed_low = normed.astype(jnp.bfloat16)
    query_low = (matmul(normed_low, query_matrix) + query_shift).astype(jnp.bfloat16)
    key_low = matmul(normed_low, key_matrix).astype(jnp.bfloat16)
    value_low = (matmul(normed_low, value_matrix) + value_shift).astype(jnp.bfloat16)
    query_low, hidden_row, first_cross = tie(query_low, hidden_row, first_cross)
    hidden_pieces += hidden_row
    beyond_pieces += first_cross
    last_cross = [links.swap(p, 2) for p in hidden_pieces[len(beyond_pieces) :]]
    inner_here, outer_here = arrange(
        sources, hidden_pieces, [(0, rows), (rows, rows)], [width, width]
    )
    inner_beside, outer_beside = links.swap(inner_here, 1), links.swap(outer_here, 1)
    context = attend_call(lengths, query_low, key_low, value_low)
    context, last_cross = tie(context, last_cross)
    beyond_pieces += last_cross
    inner_beyond, outer_beyond = arrange(
        sources, beyond_pieces, [(0, rows), (rows, rows)], [width, width]
    )
    inner_matrix = [inner_here, inner_beside, inner_beyond, links.swap(inner_beyond, 1)]
    outer_matrix = [outer_here, outer_beside, outer_beyond, links.swap(outer_beyond, 1)]
    inner_matrix = [item.reshape(width, width) for item in inner_matrix]
    outer_matrix = [item.reshape(width, width) for item in outer_matrix]
    attended = matmul(context, output_matrix) + output_shift
    middle, hat_middle, inv_middle = normalize(normed + attended, middle_scale, middle_shift)
    middle_low = middle.astype(jnp.bfloat16)
    activated, slopes, branch = hidden_call(middle_low, inner_shift, inner_matrix, outer_matrix)
    result, hat_final, inv_final = normalize(
        middle + branch + outer_shift, final_scale, final_shift
    )
    output = result.astype(jnp.bfloat16).reshape(1, full_len, width)

    upstream = cotangent.reshape(full_len, width).astype(jnp.float32)
    final_gain_gradient = jnp.sum(upstream * hat_final, axis=0)
    final_bias_gradient = jnp.sum(upstream, axis=0)
    second = normalize_back(upstream, hat_final, inv_final, final_scale)
    branch_grad = second.astype(jnp.bfloat16)
    outer_bias_gradient = jnp.sum(branch_grad.astype(jnp.float32), axis=0)

    def local_terms(left, right):
        return contract_rows(left, right).astype(jnp.bfloat16).reshape(owners, rows, width)

    outer_terms = [None] * 4
    for i in (3, 1, 2, 0):
        outer_terms[i] = local_terms(activated[i], branch_grad)
    outer_cross = [links.swap(outer_terms[i], 1) for i in (3, 1)]
    inner_grad = [
        (times_transposed(branch_grad, outer_matrix[i]) * slopes[i].astype(jnp.float32)).astype(jnp.bfloat16)
        for i in range(4)
    ]
    inner_grad, outer_cross = tie(inner_grad, outer_cross)
    outer_sent, inner_grad = tie(add(outer_terms[2], outer_cross[0]), inner_grad)
    outer_across = links.swap(outer_sent, 2)
    outer_near = add(outer_terms[0], outer_cross[1])
    inner_bias_gradient = [jnp.sum(item.astype(jnp.float32), axis=0) for item in inner_grad]
    inner_terms = [None] * 4
    for i in (3, 1, 2, 0):
        inner_terms[i] = contract_rows(middle_low, inner_grad[i]).astype(jnp.bfloat16)
        inner_terms[i] = inner_terms[i].reshape(owners, rows, width)
    inner_cross = [links.swap(inner_terms[i], 1) for i in (3, 1)]
    middle_grad = second + sum(times_transposed(inner_grad[i], inner_matrix[i]) for i in range(4))
    middle_grad, inner_cross, outer_across = tie(middle_grad, inner_cross, outer_across)
    inner_across_sent, outer_whole, middle_grad = tie(
        add(inner_terms[2], inner_cross[0]),
        links.split(add(outer_near, outer_across), 0),
        middle_grad,
    )
    inner_across = links.swap(inner_across_sent, 2)
    outer_half = links.fold_b(outer_whole, 0)
    inner_near = add(inner_terms[0], inner_cross[1])
    middle_gain_gradient = jnp.sum(middle_grad * hat_middle, axis=0)
    middle_bias_gradient = jnp.sum(middle_grad, axis=0)
    first = normalize_back(middle_grad, hat_middle, inv_middle, middle_scale)
    attended_grad = first.astype(jnp.bfloat16)
    output_bias_gradient = jnp.sum(attended_grad.astype(jnp.float32), axis=0)
    context_grad = times_transposed(attended_grad, output_matrix).astype(jnp.bfloat16)
    query_low_grad, key_low_grad, value_low_grad, query_bias_gradient, value_bias_gradient = (
        attend_back_call(lengths, query_low, key_low, value_low, context_grad)
    )
    query_low_grad, key_low_grad, value_low_grad, inner_across, outer_half = tie(
        query_low_grad, key_low_grad, value_low_grad, inner_across, outer_half
    )
    outer_share = links.fold_a(outer_half, 0)
    inner_half = links.fold_b(links.split(add(inner_near, inner_across), 0), 0)
    own_left = jnp.where(core == 0, normed_low, context)
    sent_left = jnp.where(core == 0, context, normed_low)
    square_sent = [
        local_terms(normed_low, jnp.where(core == 0, value_low_grad, query_low_grad)),
        local_terms(sent_left, jnp.where(core == 0, attended_grad, key_low_grad)),
    ]
    square_cross = [links.swap(item, 1) for item in square_sent]
    square_own = [
        local_terms(normed_low, jnp.where(core == 0, query_low_grad, value_low_grad)),
        local_terms(own_left, jnp.where(core == 0, key_low_grad, attended_grad)),
    ]
    normed_grad = (
        first
        + times_transposed(query_low_grad, query_matrix)
        + times_transposed(key_low_grad, key_matrix)
        + times_transposed(value_low_grad, value_matrix)
    )
    embed_gain_gradient = jnp.sum(normed_grad * hat_embed, axis=0)
    embed_bias_gradient = jnp.sum(normed_grad, axis=0)
    summed_grad = normalize_back(normed_grad, hat_embed, inv_embed, embed_scale)
    embedded_grad = summed_grad.astype(jnp.bfloat16)
    embedded_grad, outer_share, inner_half, square_cross = tie(
        embedded_grad, outer_share, inner_half, square_cross
    )

    wide = width // 2
    features = [embedded_grad[:, :wide], embedded_grad[:, wide:]]

    def rows_of(features):
        return jnp.einsum(
            "ts,td->sd", route, features, preferred_element_type=jnp.float32
        ).astype(jnp.bfloat16)

    kept = rows_of(jnp.where(core == 0, features[0], features[1]))
    given = links.swap(rows_of(jnp.where(core == 0, features[1], features[0])), 1)
    leaving = jnp.stack(
        [item.reshape(owners, cap, wide) for item in ordered(kept, given)], axis=1
    )
    known = jnp.stack(
        [item.reshape(owners, cap) for item in ordered(held_ids, links.swap(held_ids, 1))], axis=1
    )
    parts = 2
    cut = cap // parts
    known = known.reshape(owners, 2, parts, cut).transpose(2, 0, 1, 3).reshape(-1)
    known_sets = [known]
    bit = 2
    while bit < groups:
        known_sets += [links.swap(item, bit) for item in known_sets]
        bit *= 2
    sums = [
        embed_gain_gradient, embed_bias_gradient, query_bias_gradient, value_bias_gradient,
        output_bias_gradient, middle_gain_gradient, middle_bias_gradient, outer_bias_gradient,
        final_gain_gradient, final_bias_gradient,
    ]
    inner_bias_gradient = jnp.stack(inner_bias_gradient)[jnp.stack(blocks)]
    vector_terms = jnp.concatenate(
        [item.reshape(1, width) for item in sums] + [inner_bias_gradient]
    )
    vector_terms = vector_terms.reshape(14, owners, rows).transpose(1, 0, 2)
    vector_terms = jnp.pad(vector_terms, ((0, 0), (0, 2), (0, width - rows)))
    vector_terms = vector_terms.reshape(owners, 2, 8, width).astype(jnp.bfloat16)
    place_terms = embedded_grad.reshape(owners, 2, place_part, width)
    late_terms = jnp.concatenate([place_terms, vector_terms], axis=2)
    late_cross = links.swap(pick(late_terms, 1 - core, 1), 1)
    bits = []
    bit = 2
    while bit < groups:
        bits.append(bit)
        bit *= 2

    def exchange(part):
        piece = leaving[:, :, part * cut : (part + 1) * cut]
        return lax.all_to_all(piece, "vocab", 0, 0, tiled=True)

    def beyond(piece):
        items = [piece]
        for bit in bits:
            items = items + [links.swap(item, bit) for item in items]
        return items

    def table_term(pieces, known):
        return matmul((table_ids[:, None] == known[None, :]).astype(jnp.bfloat16), pieces)

    table_ids = lax.iota(jnp.int32, table_rows)
    landed, late_cross, leaving = tie(exchange(0).reshape(-1, wide), late_cross, leaving)
    late_whole = jnp.concatenate(
        [
            add(square_own[0], square_cross[0]),
            add(square_own[1], square_cross[1]),
            add(pick(late_terms, core, 1), late_cross),
        ],
        axis=1,
    )
    late_half = links.fold_b(links.split(late_whole, 0), 0)
    first_sets = beyond(landed)
    landed, late_half, first_sets = tie(exchange(1).reshape(-1, wide), late_half, first_sets)
    share = links.fold_a(jnp.concatenate([inner_half, late_half], axis=1), 0)
    second_sets = beyond(landed)
    table_sum = [table_term(jnp.concatenate([first_sets[0], second_sets[0]]), known_sets[0])]
    share, second_sets, table_sum = tie(share, second_sets, table_sum)
    share = links.far(jnp.concatenate([outer_share, share]), 4)
    share_beyond = links.swap(share, 2)
    for i in range(1, len(known_sets)):
        pieces = jnp.concatenate([first_sets[i], second_sets[i]])
        table_sum.append(table_term(pieces, known_sets[i]))
    while len(table_sum) > 1:
        table_sum = [a + b for a, b in zip(table_sum[::2], table_sum[1::2])]
    table_half, share_beyond = tie(table_sum[0].astype(jnp.bfloat16), share_beyond)
    late_share = add(share[2 * rows :], share_beyond[2 * rows :])
    share_core = jnp.concatenate([share[: 2 * rows], share_beyond[: 2 * rows], late_share])
    table_other, share_other = links.swap(table_half, 1), links.swap(share_core, 1)
    table_other, share_other = tie(table_other, share_other)
    table_gradient = widen_call(core, table_half, table_other)
    low_share, high_share = ordered(share_core[4 * rows :], share_other[4 * rows :])
    first_share, second_share = low_share[:rows], low_share[rows : 2 * rows]
    third_share, fourth_share = high_share[:rows], high_share[rows : 2 * rows]
    place_end = 2 * rows + place_part
    position_gradient = jnp.concatenate(
        [low_share[2 * rows : place_end], high_share[2 * rows : place_end]]
    )
    vector_share = jnp.concatenate([low_share[place_end:, :rows], high_share[place_end:, :rows]])
    vector_share = vector_share.astype(jnp.float32)
    (
        embed_gain_gradient, embed_bias_gradient, query_bias_gradient, value_bias_gradient,
        output_bias_gradient, middle_gain_gradient, middle_bias_gradient, outer_bias_gradient,
        final_gain_gradient, final_bias_gradient,
    ) = (vector_share[i] for i in range(10))
    inner_bias_gradient = vector_share[10:14].reshape(4 * rows)

    def quad(start):
        own, beside = share_core[start : start + 3 * rows], share_other[start : start + 3 * rows]
        items = [own[:rows], beside[:rows], own[2 * rows :], beside[2 * rows :]]
        return jnp.stack(items)[jnp.stack(blocks)]

    outer_weight_gradient = quad(0).reshape(4 * rows, width)
    inner_weight_gradient = quad(rows).reshape(4, rows, owners, rows)
    inner_weight_gradient = inner_weight_gradient.transpose(1, 2, 0, 3).reshape(rows, hidden)

    def wider(share):
        return share.astype(jnp.float32)

    return (
        output,
        table_gradient,
        wider(position_gradient),
        embed_gain_gradient,
        embed_bias_gradient,
        wider(first_share),
        query_bias_gradient,
        wider(second_share),
        wider(third_share),
        value_bias_gradient,
        wider(fourth_share),
        output_bias_gradient,
        middle_gain_gradient,
        middle_bias_gradient,
        wider(inner_weight_gradient),
        inner_bias_gradient,
        wider(outer_weight_gradient),
        outer_bias_gradient,
        final_gain_gradient,
        final_bias_gradient,
    )


def solution(mesh):
    return jax.shard_map(
        functools.partial(on_device, mesh.shape["dp"], mesh.shape["vocab"]),
        mesh=mesh,
        in_specs=(
            P(("dp", "vocab"), None),
            P(("dp", "vocab")),
            P("vocab", None),
            P("vocab", None),
            P("vocab"),
            P("vocab"),
            P("vocab", None),
            P("vocab"),
            P("vocab", None),
            P("vocab", None),
            P("vocab"),
            P("vocab", None),
            P("vocab"),
            P("vocab"),
            P("vocab"),
            P("vocab", None),
            P("vocab"),
            P("vocab", None),
            P("vocab"),
            P("vocab"),
            P("vocab"),
            P(("dp", "vocab"), None, None),
        ),
        out_specs=(
            P(("dp", "vocab"), None, None),
            P("vocab", None),
            P("vocab", None),
            P("vocab"),
            P("vocab"),
            P("vocab", None),
            P("vocab"),
            P("vocab", None),
            P("vocab", None),
            P("vocab"),
            P("vocab", None),
            P("vocab"),
            P("vocab"),
            P("vocab"),
            P("vocab", None),
            P("vocab"),
            P("vocab", None),
            P("vocab"),
            P("vocab"),
            P("vocab"),
        ),
        check_vma=False,
    )
```

```python
import functools
import math

import jax
import jax.numpy as jnp
from jax import lax
from jax.experimental import pallas as pl
from jax.experimental.pallas import tpu as pltpu
from jax.sharding import PartitionSpec as P

HEADS = 12


epsilon = 1e-12
scaling = 0.125


def normalize(values, gain, bias_row):
    center = values - jnp.mean(values, axis=-1, keepdims=True)
    inverse = lax.rsqrt(jnp.mean(center * center, axis=-1, keepdims=True) + epsilon)
    scaled = center * inverse
    return (scaled * gain + bias_row, scaled, inverse)


def normalize_back(upstream, scaled, inverse, gain):
    weighted = upstream * gain
    return inverse * (
        weighted
        - jnp.mean(weighted, axis=-1, keepdims=True)
        - scaled * jnp.mean(weighted * scaled, axis=-1, keepdims=True)
    )


def gelu_slope(inner):
    cumulative = 0.5 * (1.0 + lax.erf(inner * (1.0 / math.sqrt(2.0))))
    density = jnp.exp(-0.5 * inner * inner) * (1.0 / math.sqrt(2.0 * math.pi))
    return cumulative + inner * density


def matmul(left, right):
    return jnp.dot(left, right, preferred_element_type=jnp.float32)


def contract_rows(left, right):
    return jnp.einsum("ti,tj->ij", left, right, preferred_element_type=jnp.float32)


def times_transposed(left, right):
    return jnp.einsum("tj,ij->ti", left, right, preferred_element_type=jnp.float32)


def split_heads(rows):
    return rows.reshape(rows.shape[0], HEADS, rows.shape[1] // HEADS)


def masked_scores(query_heads, key_heads, visible):
    scores = (
        jnp.einsum("qhd,khd->hqk", query_heads, key_heads, preferred_element_type=jnp.float32)
        * scaling
    )
    return jnp.where(visible[None, None, :], scores, -1e30)


def attend(inputs):
    query_rows, key_rows, value_rows, visible = inputs
    query_heads = split_heads(query_rows)
    scores = masked_scores(query_heads, split_heads(key_rows), visible)
    largest = jnp.max(scores, axis=-1, keepdims=True)
    raised = jnp.exp(scores - largest)
    totals = jnp.sum(raised, axis=-1, keepdims=True)
    probs = raised / totals
    context = jnp.einsum(
        "hqk,khd->qhd",
        probs.astype(jnp.bfloat16),
        split_heads(value_rows),
        preferred_element_type=jnp.float32,
    )
    return (context.reshape(query_rows.shape).astype(jnp.bfloat16), largest + jnp.log(totals))


def attend_back(inputs):
    query_rows, key_rows, value_rows, visible, kept_lse, context_grad = inputs
    query_heads = split_heads(query_rows)
    key_heads = split_heads(key_rows)
    value_heads = split_heads(value_rows)
    grad_heads = split_heads(context_grad)
    probs = jnp.exp(masked_scores(query_heads, key_heads, visible) - kept_lse)
    prob_grad = jnp.einsum(
        "qhd,khd->hqk", grad_heads, value_heads, preferred_element_type=jnp.float32
    )
    centered = prob_grad - jnp.sum(prob_grad * probs, axis=-1, keepdims=True)
    score_grad = (probs * centered).astype(jnp.bfloat16)
    query_grad = (
        jnp.einsum("hqk,khd->qhd", score_grad, key_heads, preferred_element_type=jnp.float32)
        * scaling
    )
    key_grad = (
        jnp.einsum("hqk,qhd->khd", score_grad, query_heads, preferred_element_type=jnp.float32)
        * scaling
    )
    value_grad = jnp.einsum(
        "hqk,qhd->khd", probs.astype(jnp.bfloat16), grad_heads, preferred_element_type=jnp.float32
    )
    return (
        query_grad.reshape(query_rows.shape),
        key_grad.reshape(key_rows.shape),
        value_grad.reshape(value_rows.shape),
    )


class Links:
    def __init__(self, groups, owners):
        self.groups, self.owners = groups, owners
        self.A = 4 if owners % 4 == 0 else 1
        self.B = owners // self.A

    def place(self):
        vocab = lax.axis_index("vocab")
        return vocab // self.B, vocab % self.B

    def step_a(self, piece, far=1):
        A, B = self.A, self.B
        pairs = [(a * B + b, (a + far) % A * B + b) for a in range(A) for b in range(B)]
        return lax.ppermute(piece, "vocab", pairs)

    def step_b(self, piece):
        A, B = self.A, self.B
        pairs = [(a * B + b, a * B + (b + 1) % B) for a in range(A) for b in range(B)]
        return lax.ppermute(piece, "vocab", pairs)

    def swap(self, piece, bit):
        return lax.ppermute(piece, "dp", [(i, i ^ bit) for i in range(self.groups)])

    def row(self, piece):
        pieces = [piece]
        for _ in range(1, self.B):
            pieces.append(self.step_b(pieces[-1]))
        return pieces

    def sources(self):
        a, b = self.place()
        A, B = self.A, self.B
        return jnp.stack([(a - k + A) % A * B + (b - m + B) % B for k in range(A) for m in range(B)])

    def fold_b(self, total, axis):
        sent, kept = self.last_b(total, axis)
        return add(self.step_b(sent), kept)

    def last_b(self, total, axis):
        B = self.B
        here = self.place()[1]

        def block(index):
            return pick(total, index % B, axis + 1)

        held = block(here - 1 + B)
        for s in range(1, B - 1):
            held = add(self.step_b(held), block(here - 1 - s + 2 * B))
        return held, block(here)

    def cut_a(self, total, axis):
        here = self.place()[0]
        return [pick(total, (here + far) % self.A, axis) for far in range(self.A)]

    def sent_a(self, terms):
        return [self.step_a(terms[far], far) for far in range(1, self.A)]

    def split(self, total, axis):
        return total.reshape(total.shape[:axis] + (self.A, self.B) + total.shape[axis + 1 :])

    def far(self, piece, first):
        bit = first
        while bit < self.groups:
            piece = add(piece, self.swap(piece, bit))
            bit *= 2
        return piece


def add(*terms):
    return sum(term.astype(jnp.float32) for term in terms).astype(jnp.bfloat16)


def tie(*values):
    return lax.optimization_barrier(values)


def gelu(inner):
    return inner * (0.5 * (1.0 + lax.erf(inner * (1.0 / math.sqrt(2.0)))))


def pick(stacked, index, axis=0):
    return lax.dynamic_index_in_dim(stacked, index, axis, keepdims=False)


def arrange(sources, pieces, bands, lanes):
    owners = len(pieces)

    def body(sources_ref, *refs):
        ins, outs = refs[:owners], refs[owners:]
        for i in range(owners):
            where = sources_ref[i]
            for (start, size), wide, out in zip(bands, lanes, outs):
                out[where] = ins[i][start : start + size, :wide]

    return pl.pallas_call(
        body,
        out_shape=tuple(
            jax.ShapeDtypeStruct((owners, size, wide), pieces[0].dtype)
            for (start, size), wide in zip(bands, lanes)
        ),
        in_specs=[pl.BlockSpec(memory_space=pltpu.SMEM)]
        + [pl.BlockSpec(memory_space=pltpu.VMEM)] * owners,
        out_specs=tuple(pl.BlockSpec(memory_space=pltpu.VMEM) for _ in bands),
        cost_estimate=pl.CostEstimate(
            flops=0, bytes_accessed=4 * owners * pieces[0].size, transcendentals=0
        ),
        name="arrange",
    )(sources, *pieces)


def cost(micros):
    return pl.CostEstimate(flops=0, bytes_accessed=int(micros * 3e6), transcendentals=0)


def whole(count):
    return [pl.BlockSpec(memory_space=pltpu.VMEM)] * count


SMEM = pl.BlockSpec(memory_space=pltpu.SMEM)


def dot(left, right, dims=((1,), (0,))):
    return lax.dot_general(left, right, (dims, ((), ())), preferred_element_type=jnp.float32)


def head_masks(shape):
    low = lax.broadcasted_iota(jnp.int32, shape, 1) < shape[1] // 2
    return low, jnp.logical_not(low)


def attend_kernel(length_ref, query_ref, key_ref, value_ref, context_ref):
    count, wide = query_ref.shape[0], 2 * query_ref.shape[1] // HEADS
    hidden_keys = lax.broadcasted_iota(jnp.int32, (count, count), 1) >= length_ref[0]

    @pl.loop(0, HEADS // 2)
    def _(pair):
        lanes = pl.ds(pl.multiple_of(pair * wide, wide), wide)
        query, key, value = query_ref[:, lanes], key_ref[:, lanes], value_ref[:, lanes]
        query = query * scaling
        masks = head_masks((count, wide))
        parts = []
        for mask in masks:
            scores = dot(jnp.where(mask, query, 0).astype(jnp.bfloat16), key, ((1,), (1,)))
            scores = jnp.where(hidden_keys, -1e30, scores)
            raised = jnp.exp(scores - jnp.max(scores, axis=1, keepdims=True))
            totals = jnp.sum(raised, axis=1, keepdims=True)
            parts.append(dot(raised.astype(jnp.bfloat16), value) / totals)
        context_ref[:, lanes] = jnp.where(masks[0], parts[0], parts[1]).astype(jnp.bfloat16)


def attend_call(length, query, key, value):
    return pl.pallas_call(
        attend_kernel,
        out_shape=jax.ShapeDtypeStruct(query.shape, jnp.bfloat16),
        in_specs=[SMEM] + whole(3),
        out_specs=pl.BlockSpec(memory_space=pltpu.VMEM),
        cost_estimate=cost(4),
        name="attend",
    )(length, query, key, value)


def attend_back_kernel(
    length_ref, query_ref, key_ref, value_ref, grad_ref,
    query_grad_ref, key_grad_ref, value_grad_ref, query_sum_ref, value_sum_ref,
):
    count, wide = query_ref.shape[0], 2 * query_ref.shape[1] // HEADS
    half = wide // 2
    hidden_keys = lax.broadcasted_iota(jnp.int32, (count, count), 0) >= length_ref[0]

    @pl.loop(0, HEADS // 2)
    def _(pair):
        lanes = pl.ds(pl.multiple_of(pair * wide, wide), wide)
        query, key = query_ref[:, lanes] * scaling, key_ref[:, lanes]
        query = query.astype(jnp.bfloat16)
        value, grad = value_ref[:, lanes], grad_ref[:, lanes]
        across = jnp.transpose(key.astype(jnp.float32)).astype(jnp.bfloat16)
        masks = head_masks((count, wide))
        query_parts, key_parts, value_parts = [], [], []
        for i, mask in enumerate(masks):
            scores = dot(key, jnp.where(mask, query, 0).astype(jnp.bfloat16), ((1,), (1,)))
            scores = jnp.where(hidden_keys, -1e30, scores)
            raised = jnp.exp(scores - jnp.max(scores, axis=0, keepdims=True))
            probs = raised * (1.0 / jnp.sum(raised, axis=0, keepdims=True))
            prob_grad = dot(jnp.where(mask, value, 0).astype(jnp.bfloat16), grad, ((1,), (1,)))
            centered = prob_grad - jnp.sum(prob_grad * probs, axis=0, keepdims=True)
            score_grad = (probs * centered).astype(jnp.bfloat16)
            value_parts.append(dot(probs.astype(jnp.bfloat16), grad))
            key_parts.append(dot(score_grad, query))
            query_parts.append(dot(across[i * half : (i + 1) * half], score_grad))
        value_grad = jnp.where(masks[0], value_parts[0], value_parts[1]).astype(jnp.bfloat16)
        value_grad_ref[:, lanes] = value_grad
        value_sum_ref[:, lanes] = jnp.sum(value_grad.astype(jnp.float32), axis=0, keepdims=True)
        key_grad = jnp.where(masks[0], key_parts[0], key_parts[1])
        key_grad_ref[:, lanes] = key_grad.astype(jnp.bfloat16)
        query_grad = jnp.transpose(jnp.concatenate(query_parts, axis=0) * scaling)
        query_grad = query_grad.astype(jnp.bfloat16)
        query_grad_ref[:, lanes] = query_grad
        query_sum_ref[:, lanes] = jnp.sum(query_grad.astype(jnp.float32), axis=0, keepdims=True)


def hidden_kernel(rows_ref, shift_ref, *refs):
    inner_refs, outer_refs, active_refs, slope_refs = (refs[4 * i : 4 * i + 4] for i in range(4))
    branch_ref = refs[16]
    width = rows_ref.shape[1]
    tile = 256
    branch_ref[...] = jnp.zeros_like(branch_ref)
    for i in range(4):

        @pl.loop(0, width // tile)
        def _(part, i=i):
            lanes = pl.ds(pl.multiple_of(part * tile, tile), tile)
            inner = dot(rows_ref[...], inner_refs[i][:, lanes]) + shift_ref[i : i + 1, lanes]
            cumulative = 0.5 * (1.0 + lax.erf(inner * (1.0 / math.sqrt(2.0))))
            density = jnp.exp(-0.5 * inner * inner) * (1.0 / math.sqrt(2.0 * math.pi))
            active = (inner * cumulative).astype(jnp.bfloat16)
            active_refs[i][:, lanes] = active
            slope_refs[i][:, lanes] = (cumulative + inner * density).astype(jnp.bfloat16)
            branch_ref[...] += dot(active, outer_refs[i][lanes, :])


def hidden_call(rows, shift, inner, outer):
    like = jax.ShapeDtypeStruct(rows.shape, jnp.bfloat16)
    out = pl.pallas_call(
        hidden_kernel,
        out_shape=(like,) * 8 + (jax.ShapeDtypeStruct(rows.shape, jnp.float32),),
        in_specs=whole(10),
        out_specs=tuple(whole(9)),
        cost_estimate=cost(8),
        name="hidden",
    )(rows, shift, *inner, *outer)
    return out[:4], out[4:8], out[8]


def normed_back_kernel(first_ref, hat_ref, inverse_ref, scale_ref, *refs):
    grads, weights, (out_ref, gain_ref, bias_ref) = refs[:3], refs[3:6], refs[6:]
    upstream = first_ref[...]
    for grad, weight in zip(grads, weights):
        upstream = upstream + dot(grad[...], weight[...], ((1,), (1,)))
    hat = hat_ref[...]
    gain_ref[...] = jnp.sum(upstream * hat, axis=0, keepdims=True)
    bias_ref[...] = jnp.sum(upstream, axis=0, keepdims=True)
    out_ref[...] = normalize_back(upstream, hat, inverse_ref[...], scale_ref[...]).astype(jnp.bfloat16)


def front_back_kernel(*refs):
    attention, norm, weights, outs = refs[:5], refs[5:9], refs[9:12], refs[12:]
    attend_back_kernel(*attention, *outs[:5])
    normed_back_kernel(*norm, *outs[:3], *weights, *outs[5:])


def front_back_call(length, query, key, value, grad, first, hat, inverse, scale, weights):
    like = jax.ShapeDtypeStruct(query.shape, jnp.bfloat16)
    line = jax.ShapeDtypeStruct((1, query.shape[1]), jnp.float32)
    return pl.pallas_call(
        front_back_kernel,
        out_shape=(like, like, like, line, line, like, line, line),
        in_specs=[SMEM] + whole(11),
        out_specs=tuple(whole(8)),
        cost_estimate=cost(1),
        name="front_back",
    )(length, query, key, value, grad, first, hat, inverse, scale.reshape(1, -1), *weights)


def widen_kernel(core_ref, here_ref, there_ref, out_ref):
    wide = here_ref.shape[1]

    @pl.when(core_ref[0] == 0)
    def _():
        out_ref[:, :wide] = here_ref[...].astype(jnp.float32)
        out_ref[:, wide:] = there_ref[...].astype(jnp.float32)

    @pl.when(core_ref[0] != 0)
    def _():
        out_ref[:, :wide] = there_ref[...].astype(jnp.float32)
        out_ref[:, wide:] = here_ref[...].astype(jnp.float32)


def widen_call(core, here, there):
    count, wide = here.shape
    tile = count // 8
    return pl.pallas_call(
        widen_kernel,
        grid=(8,),
        out_shape=jax.ShapeDtypeStruct((count, 2 * wide), jnp.float32),
        in_specs=[SMEM] + [pl.BlockSpec((tile, wide), lambda i: (i, 0))] * 2,
        out_specs=pl.BlockSpec((tile, 2 * wide), lambda i: (i, 0)),
        cost_estimate=cost(5),
        name="widen",
    )(core.reshape(1), here, there)


def on_device(
    groups,
    owners,
    token_ids,
    lengths,
    word_table,
    position_table,
    embed_gain,
    embed_bias,
    query_weight,
    query_bias,
    key_weight,
    value_weight,
    value_bias,
    output_weight,
    output_bias,
    middle_gain,
    middle_bias,
    inner_weight,
    inner_bias,
    outer_weight,
    outer_bias,
    final_gain,
    final_bias,
    cotangent,
):
    links = Links(groups, owners)
    table_rows, width = word_table.shape
    full_len = token_ids.shape[1]
    rows = query_weight.shape[0]
    hidden = inner_weight.shape[1]
    cap = 2 * full_len // owners
    place_part = position_table.shape[0] // 2
    dp = lax.axis_index("dp")
    core, quarter = dp % 2, dp % 4
    blocks = [quarter, quarter ^ 1, quarter ^ 2, quarter ^ 3]
    ids = token_ids.reshape(full_len)

    inner_quarter = pick(inner_weight.reshape(rows, owners, 4, rows), quarter, 2)
    hidden_piece = jnp.concatenate(
        [
            inner_quarter.reshape(rows, width),
            lax.dynamic_slice_in_dim(outer_weight, quarter * rows, rows, 0),
        ]
    )
    vectors = [
        embed_gain, embed_bias, query_bias, value_bias, output_bias, middle_gain, middle_bias,
        outer_bias, final_gain, final_bias,
    ]
    vectors += [inner_bias[i * rows : (i + 1) * rows] for i in range(4)]
    vector_piece = sum(
        lax.pad(
            item.reshape(1, rows),
            jnp.zeros((), jnp.bfloat16),
            ((i, 15 - i, 0), (0, width - rows, 0)),
        )
        for i, item in enumerate(vectors)
    )
    square_piece = jnp.concatenate(
        [
            jnp.where(core == 0, query_weight, value_weight),
            jnp.where(core == 0, key_weight, output_weight),
            lax.dynamic_slice_in_dim(position_table, core * place_part, place_part, 0),
            vector_piece,
        ]
    )

    owner = ids // table_rows
    local = ids - owner * table_rows
    onehot = owner[:, None] == lax.iota(jnp.int32, owners)[None, :]
    before = lax.iota(jnp.int32, full_len)
    lower = (before[:, None] > before[None, :]).astype(jnp.bfloat16)
    ranks = matmul(lower, onehot.astype(jnp.bfloat16))
    rank = jnp.sum(jnp.where(onehot, ranks, 0.0), axis=1).astype(jnp.int32)
    slot = owner * cap + rank
    slots = lax.iota(jnp.int32, owners * cap)
    sent_ids = jnp.sum(
        jnp.where(slots[:, None] == slot[None, :], local[None, :] + 1, 0), axis=1
    ) - 1
    held_ids = lax.all_to_all(sent_ids.reshape(owners, cap), "vocab", 0, 0, tiled=True).reshape(-1)

    picked = jnp.take(word_table, jnp.maximum(held_ids, 0), axis=0)
    hidden_pieces, square_pieces, beyond_pieces = [], [], []
    hidden_held, square_held = hidden_piece, square_piece
    A = links.A
    plan = [(0, 0, None), (1, None, 0), (2, 1, None), (3, 2, 1)]
    if A == 1:
        plan = [(0, None, None)]
    arrived = None
    for square_step, hidden_step, cross in plan:
        square_row = links.row(square_held)
        square_next = links.step_a(square_held) if square_step < A - 1 else ()
        hidden_row, hidden_next, crossing = (), (), ()
        if hidden_step is not None:
            hidden_row, hidden_next = links.row(hidden_held), links.step_a(hidden_held)
        if cross is not None:
            here = slice(cross * links.B, (cross + 1) * links.B)
            crossing = [links.swap(piece, 2) for piece in hidden_pieces[here]]
        tied = tie(square_row, square_next, hidden_row, hidden_next, crossing, picked)
        square_row, square_next, hidden_row, hidden_next, crossing, picked = tied
        square_pieces += square_row
        hidden_pieces += hidden_row
        beyond_pieces += crossing
        square_held = square_next
        if hidden_step is not None:
            hidden_held = hidden_next
        if arrived is None:
            arrived = lax.all_to_all(
                picked.reshape(owners, cap, width), "vocab", 0, 0, tiled=True
            )
    sources = links.sources()
    first_here, second_here, place_here, small = arrange(
        sources,
        square_pieces,
        [(0, rows), (rows, rows), (2 * rows, place_part), (2 * rows + place_part, 16)],
        [width, width, width, 128 * -(-rows // 128)],
    )
    first_there, second_there, place_there = (
        links.swap(item, 1) for item in (first_here, second_here, place_here)
    )
    hidden_row = links.row(hidden_held)
    first_cross = [links.swap(p, 2) for p in hidden_pieces[len(beyond_pieces) :]]

    small = jnp.transpose(small[:, :, :rows], (1, 0, 2)).reshape(16, width).astype(jnp.float32)
    (
        embed_scale, embed_shift, query_shift, value_shift, output_shift, middle_scale,
        middle_shift, outer_shift, final_scale, final_shift,
    ) = (small[i] for i in range(10))
    inner_shift = jnp.stack([pick(small, 10 + i) for i in blocks])

    def ordered(here, there):
        return jnp.where(core == 0, here, there), jnp.where(core == 0, there, here)

    query_matrix, value_matrix = ordered(
        first_here.reshape(width, width), first_there.reshape(width, width)
    )
    key_matrix, output_matrix = ordered(
        second_here.reshape(width, width), second_there.reshape(width, width)
    )
    place_rows = jnp.stack(ordered(place_here, place_there), axis=1).reshape(full_len, width)

    route = (slot[:, None] == slots[None, :]).astype(jnp.bfloat16)
    embedded = matmul(route, arrived.reshape(owners * cap, width))
    summed = embedded + place_rows.astype(jnp.float32)
    normed, hat_embed, inv_embed = normalize(summed, embed_scale, embed_shift)
    normed_low = normed.astype(jnp.bfloat16)
    query_low = (matmul(normed_low, query_matrix) + query_shift).astype(jnp.bfloat16)
    key_low = matmul(normed_low, key_matrix).astype(jnp.bfloat16)
    value_low = (matmul(normed_low, value_matrix) + value_shift).astype(jnp.bfloat16)
    query_low, hidden_row, first_cross = tie(query_low, hidden_row, first_cross)
    hidden_pieces += hidden_row
    beyond_pieces += first_cross
    last_cross = [links.swap(p, 2) for p in hidden_pieces[len(beyond_pieces) :]]
    inner_here, outer_here = arrange(
        sources, hidden_pieces, [(0, rows), (rows, rows)], [width, width]
    )
    inner_beside, outer_beside = links.swap(inner_here, 1), links.swap(outer_here, 1)
    context = attend_call(lengths, query_low, key_low, value_low)
    context, last_cross = tie(context, last_cross)
    beyond_pieces += last_cross
    inner_beyond, outer_beyond = arrange(
        sources, beyond_pieces, [(0, rows), (rows, rows)], [width, width]
    )
    inner_matrix = [inner_here, inner_beside, inner_beyond, links.swap(inner_beyond, 1)]
    outer_matrix = [outer_here, outer_beside, outer_beyond, links.swap(outer_beyond, 1)]
    inner_matrix = [item.reshape(width, width) for item in inner_matrix]
    outer_matrix = [item.reshape(width, width) for item in outer_matrix]
    attended = matmul(context, output_matrix) + output_shift
    middle, hat_middle, inv_middle = normalize(normed + attended, middle_scale, middle_shift)
    middle_low = middle.astype(jnp.bfloat16)
    activated, slopes, branch = hidden_call(middle_low, inner_shift, inner_matrix, outer_matrix)
    result, hat_final, inv_final = normalize(
        middle + branch + outer_shift, final_scale, final_shift
    )
    output = result.astype(jnp.bfloat16).reshape(1, full_len, width)

    upstream = cotangent.reshape(full_len, width).astype(jnp.float32)
    final_gain_gradient = jnp.sum(upstream * hat_final, axis=0)
    final_bias_gradient = jnp.sum(upstream, axis=0)
    second = normalize_back(upstream, hat_final, inv_final, final_scale)
    branch_grad = second.astype(jnp.bfloat16)
    outer_bias_gradient = jnp.sum(branch_grad.astype(jnp.float32), axis=0)

    def local_terms(left, right):
        return contract_rows(left, right).astype(jnp.bfloat16).reshape(owners, rows, width)

    outer_terms = [None] * 4
    for i in (3, 1, 2, 0):
        outer_terms[i] = local_terms(activated[i], branch_grad)
    outer_cross = [links.swap(outer_terms[i], 1) for i in (3, 1)]
    inner_grad = [
        (times_transposed(branch_grad, outer_matrix[i]) * slopes[i].astype(jnp.float32)).astype(jnp.bfloat16)
        for i in range(4)
    ]
    inner_grad, outer_cross = tie(inner_grad, outer_cross)
    outer_pair = jnp.concatenate(
        [add(outer_terms[0], outer_cross[1]), add(outer_terms[2], outer_cross[0])], axis=1
    )
    outer_pair, inner_grad = tie(links.split(outer_pair, 0), inner_grad)
    inner_bias_gradient = [jnp.sum(item.astype(jnp.float32), axis=0) for item in inner_grad]
    inner_terms = [None] * 4
    for i in (3, 1, 2, 0):
        inner_terms[i] = contract_rows(middle_low, inner_grad[i]).astype(jnp.bfloat16)
        inner_terms[i] = inner_terms[i].reshape(owners, rows, width)
    inner_cross = [links.swap(inner_terms[i], 1) for i in (3, 1)]
    middle_grad = second + sum(times_transposed(inner_grad[i], inner_matrix[i]) for i in range(4))
    middle_grad, inner_cross = tie(middle_grad, inner_cross)
    inner_sent, middle_grad = tie(add(inner_terms[2], inner_cross[0]), middle_grad)
    inner_near = add(inner_terms[0], inner_cross[1])
    middle_gain_gradient = jnp.sum(middle_grad * hat_middle, axis=0)
    middle_bias_gradient = jnp.sum(middle_grad, axis=0)
    first = normalize_back(middle_grad, hat_middle, inv_middle, middle_scale)
    attended_grad = first.astype(jnp.bfloat16)
    output_bias_gradient = jnp.sum(attended_grad.astype(jnp.float32), axis=0)
    context_grad = times_transposed(attended_grad, output_matrix).astype(jnp.bfloat16)
    outer_sent, outer_kept = links.last_b(outer_pair, 0)
    context_grad, inner_sent, outer_sent = tie(context_grad, inner_sent, outer_sent)
    inner_across = links.swap(inner_sent, 2)
    outer_held = links.step_b(outer_sent)
    back = front_back_call(
        lengths, query_low, key_low, value_low, context_grad, first, hat_embed, inv_embed,
        embed_scale, (query_matrix, key_matrix, value_matrix),
    )
    back, inner_across, outer_held = tie(back, inner_across, outer_held)
    (
        query_low_grad, key_low_grad, value_low_grad, query_bias_gradient, value_bias_gradient,
        embedded_grad, embed_gain_gradient, embed_bias_gradient,
    ) = back
    own_left = jnp.where(core == 0, normed_low, context)
    sent_left = jnp.where(core == 0, context, normed_low)
    square_sent = [
        local_terms(normed_low, jnp.where(core == 0, value_low_grad, query_low_grad)),
        local_terms(sent_left, jnp.where(core == 0, attended_grad, key_low_grad)),
    ]
    square_own = [
        local_terms(normed_low, jnp.where(core == 0, query_low_grad, value_low_grad)),
        local_terms(own_left, jnp.where(core == 0, key_low_grad, attended_grad)),
    ]
    square_cross = [links.swap(item, 1) for item in square_sent]
    outer_half = add(outer_held, outer_kept)
    outer_across = links.swap(outer_half[:, rows:], 2)
    inner_half = links.fold_b(links.split(add(inner_near, inner_across), 0), 0)
    wide = width // 2
    leaving = jnp.einsum("ts,td->sd", route, embedded_grad, preferred_element_type=jnp.float32)
    leaving = leaving.astype(jnp.bfloat16).reshape(owners, cap, width)
    parts = 2
    cut = cap // parts
    known = jnp.stack(
        [
            item.reshape(owners, parts, cut).transpose(1, 0, 2)
            for item in (held_ids, links.swap(held_ids, 1))
        ],
        axis=1,
    ).reshape(-1)
    known_sets = [known]
    bit = 2
    while bit < groups:
        known_sets += [links.swap(item, bit) for item in known_sets]
        bit *= 2
    sums = [
        embed_gain_gradient, embed_bias_gradient, query_bias_gradient, value_bias_gradient,
        output_bias_gradient, middle_gain_gradient, middle_bias_gradient, outer_bias_gradient,
        final_gain_gradient, final_bias_gradient,
    ]
    inner_bias_gradient = jnp.stack(inner_bias_gradient)[jnp.stack(blocks)]
    vector_terms = jnp.concatenate(
        [item.reshape(1, width) for item in sums] + [inner_bias_gradient]
    )
    vector_terms = vector_terms.reshape(14, owners, rows).transpose(1, 0, 2)
    vector_terms = jnp.pad(vector_terms, ((0, 0), (0, 2), (0, width - rows)))
    vector_terms = vector_terms.reshape(owners, 2, 8, width).astype(jnp.bfloat16)
    place_terms = embedded_grad.reshape(owners, 2, place_part, width)
    late_terms = jnp.concatenate([place_terms, vector_terms], axis=2)
    late_cross = links.swap(pick(late_terms, 1 - core, 1), 1)
    bits = []
    bit = 2
    while bit < groups:
        bits.append(bit)
        bit *= 2

    def exchange(part):
        piece = leaving[:, part * cut : (part + 1) * cut]
        return lax.all_to_all(piece, "vocab", 0, 0, tiled=True)

    def beyond(landed):
        landed = landed.reshape(-1, width)
        mine, theirs = ordered(landed[:, :wide], landed[:, wide:])
        items = [jnp.concatenate([mine, links.swap(theirs, 1)])]
        for bit in bits:
            items = items + [links.swap(item, bit) for item in items]
        return items

    def table_term(pieces, known):
        return matmul((table_ids[:, None] == known[None, :]).astype(jnp.bfloat16), pieces)

    table_ids = lax.iota(jnp.int32, table_rows)
    late_whole = jnp.concatenate(
        [
            add(square_own[0], square_cross[0]),
            add(square_own[1], square_cross[1]),
            add(pick(late_terms, core, 1), late_cross),
        ],
        axis=1,
    )
    landed, late_whole, leaving, outer_across, inner_half = tie(
        exchange(0), links.split(late_whole, 0), leaving, outer_across, inner_half
    )
    late_half = links.fold_b(late_whole, 0)
    first_sets = beyond(landed)
    outer_cut = links.cut_a(add(outer_half[:, :rows], outer_across), 0)
    outer_arrived = links.sent_a(outer_cut)
    landed, first_sets, outer_arrived = tie(exchange(1), first_sets, outer_arrived)
    inner_cut = links.cut_a(inner_half, 0)
    inner_arrived = links.sent_a(inner_cut)
    second_sets = beyond(landed)
    table_sum = [table_term(jnp.concatenate([first_sets[0], second_sets[0]]), known_sets[0])]
    table_sum, late_half, second_sets, inner_arrived = tie(
        table_sum, late_half, second_sets, inner_arrived
    )
    late_cut = links.cut_a(late_half, 0)
    late_arrived = links.sent_a(late_cut)
    hidden_share = jnp.concatenate(
        [add(outer_cut[0], *outer_arrived), add(inner_cut[0], *inner_arrived)]
    )
    hidden_share = links.far(hidden_share, 4)
    hidden_beyond = links.swap(hidden_share, 2)
    for i in range(1, len(known_sets)):
        pieces = jnp.concatenate([first_sets[i], second_sets[i]])
        table_sum.append(table_term(pieces, known_sets[i]))
    while len(table_sum) > 1:
        table_sum = [a + b for a, b in zip(table_sum[::2], table_sum[1::2])]
    table_half, hidden_beyond, late_arrived = tie(
        table_sum[0].astype(jnp.bfloat16), hidden_beyond, late_arrived
    )
    late_share = add(late_cut[0], *late_arrived)
    hidden_core = jnp.concatenate([hidden_share, hidden_beyond])
    hidden_other = links.swap(hidden_core, 1)
    table_other = links.swap(table_half, 1)
    late_share = links.far(late_share, 2)
    late_other = links.swap(late_share, 1)
    table_gradient = widen_call(core, table_half, table_other)
    low_share, high_share = ordered(late_share, late_other)
    first_share, second_share = low_share[:rows], low_share[rows : 2 * rows]
    third_share, fourth_share = high_share[:rows], high_share[rows : 2 * rows]
    place_end = 2 * rows + place_part
    position_gradient = jnp.concatenate(
        [low_share[2 * rows : place_end], high_share[2 * rows : place_end]]
    )
    vector_share = jnp.concatenate([low_share[place_end:, :rows], high_share[place_end:, :rows]])
    vector_share = vector_share.astype(jnp.float32)
    (
        embed_gain_gradient, embed_bias_gradient, query_bias_gradient, value_bias_gradient,
        output_bias_gradient, middle_gain_gradient, middle_bias_gradient, outer_bias_gradient,
        final_gain_gradient, final_bias_gradient,
    ) = (vector_share[i] for i in range(10))
    inner_bias_gradient = vector_share[10:14].reshape(4 * rows)

    def quad(start):
        own, beside = hidden_core[start : start + 3 * rows], hidden_other[start : start + 3 * rows]
        items = [own[:rows], beside[:rows], own[2 * rows :], beside[2 * rows :]]
        return jnp.stack(items)[jnp.stack(blocks)]

    outer_weight_gradient = quad(0).reshape(4 * rows, width)
    inner_weight_gradient = quad(rows).reshape(4, rows, owners, rows)
    inner_weight_gradient = inner_weight_gradient.transpose(1, 2, 0, 3).reshape(rows, hidden)

    def wider(share):
        return share.astype(jnp.float32)

    return (
        output,
        table_gradient,
        wider(position_gradient),
        embed_gain_gradient,
        embed_bias_gradient,
        wider(first_share),
        query_bias_gradient,
        wider(second_share),
        wider(third_share),
        value_bias_gradient,
        wider(fourth_share),
        output_bias_gradient,
        middle_gain_gradient,
        middle_bias_gradient,
        wider(inner_weight_gradient),
        inner_bias_gradient,
        wider(outer_weight_gradient),
        outer_bias_gradient,
        final_gain_gradient,
        final_bias_gradient,
    )


def solution(mesh):
    return jax.shard_map(
        functools.partial(on_device, mesh.shape["dp"], mesh.shape["vocab"]),
        mesh=mesh,
        in_specs=(
            P(("dp", "vocab"), None),
            P(("dp", "vocab")),
            P("vocab", None),
            P("vocab", None),
            P("vocab"),
            P("vocab"),
            P("vocab", None),
            P("vocab"),
            P("vocab", None),
            P("vocab", None),
            P("vocab"),
            P("vocab", None),
            P("vocab"),
            P("vocab"),
            P("vocab"),
            P("vocab", None),
            P("vocab"),
            P("vocab", None),
            P("vocab"),
            P("vocab"),
            P("vocab"),
            P(("dp", "vocab"), None, None),
        ),
        out_specs=(
            P(("dp", "vocab"), None, None),
            P("vocab", None),
            P("vocab", None),
            P("vocab"),
            P("vocab"),
            P("vocab", None),
            P("vocab"),
            P("vocab", None),
            P("vocab", None),
            P("vocab"),
            P("vocab", None),
            P("vocab"),
            P("vocab"),
            P("vocab"),
            P("vocab", None),
            P("vocab"),
            P("vocab", None),
            P("vocab"),
            P("vocab"),
            P("vocab"),
        ),
        check_vma=False,
    )
```

```python
import functools
import math

import jax
import jax.numpy as jnp
from jax import lax
from jax.experimental import pallas as pl
from jax.experimental.pallas import tpu as pltpu
from jax.sharding import PartitionSpec as P

HEADS = 12


epsilon = 1e-12
scaling = 0.125


def normalize(values, gain, bias_row):
    center = values - jnp.mean(values, axis=-1, keepdims=True)
    inverse = lax.rsqrt(jnp.mean(center * center, axis=-1, keepdims=True) + epsilon)
    scaled = center * inverse
    return (scaled * gain + bias_row, scaled, inverse)


def normalize_back(upstream, scaled, inverse, gain):
    weighted = upstream * gain
    return inverse * (
        weighted
        - jnp.mean(weighted, axis=-1, keepdims=True)
        - scaled * jnp.mean(weighted * scaled, axis=-1, keepdims=True)
    )


def gelu_slope(inner):
    cumulative = 0.5 * (1.0 + lax.erf(inner * (1.0 / math.sqrt(2.0))))
    density = jnp.exp(-0.5 * inner * inner) * (1.0 / math.sqrt(2.0 * math.pi))
    return cumulative + inner * density


def matmul(left, right):
    return jnp.dot(left, right, preferred_element_type=jnp.float32)


def contract_rows(left, right):
    return jnp.einsum("ti,tj->ij", left, right, preferred_element_type=jnp.float32)


def times_transposed(left, right):
    return jnp.einsum("tj,ij->ti", left, right, preferred_element_type=jnp.float32)


def split_heads(rows):
    return rows.reshape(rows.shape[0], HEADS, rows.shape[1] // HEADS)


def masked_scores(query_heads, key_heads, visible):
    scores = (
        jnp.einsum("qhd,khd->hqk", query_heads, key_heads, preferred_element_type=jnp.float32)
        * scaling
    )
    return jnp.where(visible[None, None, :], scores, -1e30)


def attend(inputs):
    query_rows, key_rows, value_rows, visible = inputs
    query_heads = split_heads(query_rows)
    scores = masked_scores(query_heads, split_heads(key_rows), visible)
    largest = jnp.max(scores, axis=-1, keepdims=True)
    raised = jnp.exp(scores - largest)
    totals = jnp.sum(raised, axis=-1, keepdims=True)
    probs = raised / totals
    context = jnp.einsum(
        "hqk,khd->qhd",
        probs.astype(jnp.bfloat16),
        split_heads(value_rows),
        preferred_element_type=jnp.float32,
    )
    return (context.reshape(query_rows.shape).astype(jnp.bfloat16), largest + jnp.log(totals))


def attend_back(inputs):
    query_rows, key_rows, value_rows, visible, kept_lse, context_grad = inputs
    query_heads = split_heads(query_rows)
    key_heads = split_heads(key_rows)
    value_heads = split_heads(value_rows)
    grad_heads = split_heads(context_grad)
    probs = jnp.exp(masked_scores(query_heads, key_heads, visible) - kept_lse)
    prob_grad = jnp.einsum(
        "qhd,khd->hqk", grad_heads, value_heads, preferred_element_type=jnp.float32
    )
    centered = prob_grad - jnp.sum(prob_grad * probs, axis=-1, keepdims=True)
    score_grad = (probs * centered).astype(jnp.bfloat16)
    query_grad = (
        jnp.einsum("hqk,khd->qhd", score_grad, key_heads, preferred_element_type=jnp.float32)
        * scaling
    )
    key_grad = (
        jnp.einsum("hqk,qhd->khd", score_grad, query_heads, preferred_element_type=jnp.float32)
        * scaling
    )
    value_grad = jnp.einsum(
        "hqk,qhd->khd", probs.astype(jnp.bfloat16), grad_heads, preferred_element_type=jnp.float32
    )
    return (
        query_grad.reshape(query_rows.shape),
        key_grad.reshape(key_rows.shape),
        value_grad.reshape(value_rows.shape),
    )


class Links:
    def __init__(self, groups, owners):
        self.groups, self.owners = groups, owners
        self.A = 4 if owners % 4 == 0 else 1
        self.B = owners // self.A

    def place(self):
        vocab = lax.axis_index("vocab")
        return vocab // self.B, vocab % self.B

    def step_a(self, piece, far=1):
        A, B = self.A, self.B
        pairs = [(a * B + b, (a + far) % A * B + b) for a in range(A) for b in range(B)]
        return lax.ppermute(piece, "vocab", pairs)

    def step_b(self, piece):
        A, B = self.A, self.B
        pairs = [(a * B + b, a * B + (b + 1) % B) for a in range(A) for b in range(B)]
        return lax.ppermute(piece, "vocab", pairs)

    def swap(self, piece, bit):
        return lax.ppermute(piece, "dp", [(i, i ^ bit) for i in range(self.groups)])

    def row(self, piece):
        pieces = [piece]
        for _ in range(1, self.B):
            pieces.append(self.step_b(pieces[-1]))
        return pieces

    def sources(self):
        a, b = self.place()
        A, B = self.A, self.B
        return jnp.stack([(a - k + A) % A * B + (b - m + B) % B for k in range(A) for m in range(B)])

    def fold_b(self, total, axis):
        sent, kept = self.last_b(total, axis)
        return add(self.step_b(sent), kept)

    def last_b(self, total, axis):
        B = self.B
        here = self.place()[1]

        def block(index):
            return pick(total, index % B, axis + 1)

        held = block(here - 1 + B)
        for s in range(1, B - 1):
            held = add(self.step_b(held), block(here - 1 - s + 2 * B))
        return held, block(here)

    def cut_a(self, total, axis):
        here = self.place()[0]
        return [pick(total, (here + far) % self.A, axis) for far in range(self.A)]

    def sent_a(self, terms):
        return [self.step_a(terms[far], far) for far in range(1, self.A)]

    def split(self, total, axis):
        return total.reshape(total.shape[:axis] + (self.A, self.B) + total.shape[axis + 1 :])

    def far(self, piece, first):
        bit = first
        while bit < self.groups:
            piece = add(piece, self.swap(piece, bit))
            bit *= 2
        return piece


def add(*terms):
    return sum(term.astype(jnp.float32) for term in terms).astype(jnp.bfloat16)


def tie(*values):
    return lax.optimization_barrier(values)


def gelu(inner):
    return inner * (0.5 * (1.0 + lax.erf(inner * (1.0 / math.sqrt(2.0)))))


def pick(stacked, index, axis=0):
    return lax.dynamic_index_in_dim(stacked, index, axis, keepdims=False)


def arrange(sources, pieces, bands, lanes):
    owners = len(pieces)

    def body(sources_ref, *refs):
        ins, outs = refs[:owners], refs[owners:]
        for i in range(owners):
            where = sources_ref[i]
            for (start, size), wide, out in zip(bands, lanes, outs):
                out[where] = ins[i][start : start + size, :wide]

    return pl.pallas_call(
        body,
        out_shape=tuple(
            jax.ShapeDtypeStruct((owners, size, wide), pieces[0].dtype)
            for (start, size), wide in zip(bands, lanes)
        ),
        in_specs=[pl.BlockSpec(memory_space=pltpu.SMEM)]
        + [pl.BlockSpec(memory_space=pltpu.VMEM)] * owners,
        out_specs=tuple(pl.BlockSpec(memory_space=pltpu.VMEM) for _ in bands),
        cost_estimate=pl.CostEstimate(
            flops=0, bytes_accessed=4 * owners * pieces[0].size, transcendentals=0
        ),
        name="arrange",
    )(sources, *pieces)


def cost(micros):
    return pl.CostEstimate(flops=0, bytes_accessed=int(micros * 3e6), transcendentals=0)


def whole(count):
    return [pl.BlockSpec(memory_space=pltpu.VMEM)] * count


SMEM = pl.BlockSpec(memory_space=pltpu.SMEM)


def dot(left, right, dims=((1,), (0,))):
    return lax.dot_general(left, right, (dims, ((), ())), preferred_element_type=jnp.float32)


def head_masks(shape):
    low = lax.broadcasted_iota(jnp.int32, shape, 1) < shape[1] // 2
    return low, jnp.logical_not(low)


def project_kernel(
    core_ref, rows_ref, first_here, first_there, second_here, second_there, query_shift, value_shift,
    query_ref, key_ref, value_ref,
):
    rows = rows_ref[...]

    def fill(query, key, value):
        query_ref[...] = (dot(rows, query[...]) + query_shift[...]).astype(jnp.bfloat16)
        key_ref[...] = dot(rows, key[...]).astype(jnp.bfloat16)
        value_ref[...] = (dot(rows, value[...]) + value_shift[...]).astype(jnp.bfloat16)

    @pl.when(core_ref[0] == 0)
    def _():
        fill(first_here, second_here, first_there)

    @pl.when(core_ref[0] != 0)
    def _():
        fill(first_there, second_there, first_here)


def project_call(core, rows, matrices, query_shift, value_shift):
    like = jax.ShapeDtypeStruct(rows.shape, jnp.bfloat16)
    return pl.pallas_call(
        project_kernel,
        out_shape=(like, like, like),
        in_specs=[SMEM] + whole(7),
        out_specs=tuple(whole(3)),
        cost_estimate=cost(4),
        name="project",
    )(core.reshape(1), rows, *matrices, query_shift.reshape(1, -1), value_shift.reshape(1, -1))


def attend_kernel(length_ref, query_ref, key_ref, value_ref, context_ref):
    count, wide = query_ref.shape[0], 2 * query_ref.shape[1] // HEADS
    hidden_keys = lax.broadcasted_iota(jnp.int32, (count, count), 1) >= length_ref[0]

    @pl.loop(0, HEADS // 2)
    def _(pair):
        lanes = pl.ds(pl.multiple_of(pair * wide, wide), wide)
        query, key, value = query_ref[:, lanes], key_ref[:, lanes], value_ref[:, lanes]
        query = query * scaling
        masks = head_masks((count, wide))
        parts = []
        for mask in masks:
            scores = dot(jnp.where(mask, query, 0).astype(jnp.bfloat16), key, ((1,), (1,)))
            scores = jnp.where(hidden_keys, -1e30, scores)
            raised = jnp.exp(scores - jnp.max(scores, axis=1, keepdims=True))
            totals = jnp.sum(raised, axis=1, keepdims=True)
            parts.append(dot(raised.astype(jnp.bfloat16), value) / totals)
        context_ref[:, lanes] = jnp.where(masks[0], parts[0], parts[1]).astype(jnp.bfloat16)


def attend_call(length, query, key, value):
    return pl.pallas_call(
        attend_kernel,
        out_shape=jax.ShapeDtypeStruct(query.shape, jnp.bfloat16),
        in_specs=[SMEM] + whole(3),
        out_specs=pl.BlockSpec(memory_space=pltpu.VMEM),
        cost_estimate=cost(4),
        name="attend",
    )(length, query, key, value)


def attend_back_kernel(
    length_ref, query_ref, key_ref, value_ref, grad_ref,
    query_grad_ref, key_grad_ref, value_grad_ref, query_sum_ref, value_sum_ref,
):
    count, wide = query_ref.shape[0], 2 * query_ref.shape[1] // HEADS
    half = wide // 2
    hidden_keys = lax.broadcasted_iota(jnp.int32, (count, count), 0) >= length_ref[0]

    @pl.loop(0, HEADS // 2)
    def _(pair):
        lanes = pl.ds(pl.multiple_of(pair * wide, wide), wide)
        query, key = query_ref[:, lanes] * scaling, key_ref[:, lanes]
        query = query.astype(jnp.bfloat16)
        value, grad = value_ref[:, lanes], grad_ref[:, lanes]
        across = jnp.transpose(key.astype(jnp.float32)).astype(jnp.bfloat16)
        masks = head_masks((count, wide))
        query_parts, key_parts, value_parts = [], [], []
        for i, mask in enumerate(masks):
            scores = dot(key, jnp.where(mask, query, 0).astype(jnp.bfloat16), ((1,), (1,)))
            scores = jnp.where(hidden_keys, -1e30, scores)
            raised = jnp.exp(scores - jnp.max(scores, axis=0, keepdims=True))
            probs = raised * (1.0 / jnp.sum(raised, axis=0, keepdims=True))
            prob_grad = dot(jnp.where(mask, value, 0).astype(jnp.bfloat16), grad, ((1,), (1,)))
            centered = prob_grad - jnp.sum(prob_grad * probs, axis=0, keepdims=True)
            score_grad = (probs * centered).astype(jnp.bfloat16)
            value_parts.append(dot(probs.astype(jnp.bfloat16), grad))
            key_parts.append(dot(score_grad, query))
            query_parts.append(dot(across[i * half : (i + 1) * half], score_grad))
        value_grad = jnp.where(masks[0], value_parts[0], value_parts[1]).astype(jnp.bfloat16)
        value_grad_ref[:, lanes] = value_grad
        value_sum_ref[:, lanes] = jnp.sum(value_grad.astype(jnp.float32), axis=0, keepdims=True)
        key_grad = jnp.where(masks[0], key_parts[0], key_parts[1])
        key_grad_ref[:, lanes] = key_grad.astype(jnp.bfloat16)
        query_grad = jnp.transpose(jnp.concatenate(query_parts, axis=0) * scaling)
        query_grad = query_grad.astype(jnp.bfloat16)
        query_grad_ref[:, lanes] = query_grad
        query_sum_ref[:, lanes] = jnp.sum(query_grad.astype(jnp.float32), axis=0, keepdims=True)


def hidden_kernel(rows_ref, shift_ref, *refs):
    inner_refs, outer_refs, active_refs, slope_refs = (refs[4 * i : 4 * i + 4] for i in range(4))
    branch_ref = refs[16]
    width = rows_ref.shape[1]
    tile = 256
    branch_ref[...] = jnp.zeros_like(branch_ref)
    for i in range(4):

        @pl.loop(0, width // tile)
        def _(part, i=i):
            lanes = pl.ds(pl.multiple_of(part * tile, tile), tile)
            inner = dot(rows_ref[...], inner_refs[i][:, lanes]) + shift_ref[i : i + 1, lanes]
            cumulative = 0.5 * (1.0 + lax.erf(inner * (1.0 / math.sqrt(2.0))))
            density = jnp.exp(-0.5 * inner * inner) * (1.0 / math.sqrt(2.0 * math.pi))
            active = (inner * cumulative).astype(jnp.bfloat16)
            active_refs[i][:, lanes] = active
            slope_refs[i][:, lanes] = (cumulative + inner * density).astype(jnp.bfloat16)
            branch_ref[...] += dot(active, outer_refs[i][lanes, :])


def hidden_call(rows, shift, inner, outer):
    like = jax.ShapeDtypeStruct(rows.shape, jnp.bfloat16)
    out = pl.pallas_call(
        hidden_kernel,
        out_shape=(like,) * 8 + (jax.ShapeDtypeStruct(rows.shape, jnp.float32),),
        in_specs=whole(10),
        out_specs=tuple(whole(9)),
        cost_estimate=cost(8),
        name="hidden",
    )(rows, shift, *inner, *outer)
    return out[:4], out[4:8], out[8]


def normed_back_kernel(first_ref, hat_ref, inverse_ref, scale_ref, *refs):
    grads, weights, (out_ref, gain_ref, bias_ref) = refs[:3], refs[3:6], refs[6:]
    upstream = first_ref[...]
    for grad, weight in zip(grads, weights):
        upstream = upstream + dot(grad[...], weight[...], ((1,), (1,)))
    hat = hat_ref[...]
    gain_ref[...] = jnp.sum(upstream * hat, axis=0, keepdims=True)
    bias_ref[...] = jnp.sum(upstream, axis=0, keepdims=True)
    out_ref[...] = normalize_back(upstream, hat, inverse_ref[...], scale_ref[...]).astype(jnp.bfloat16)


def front_back_kernel(*refs):
    core_ref, refs = refs[0], refs[1:]
    attention, norm, outs = refs[:5], refs[5:9], refs[13:]
    first_here, first_there, second_here, second_there = refs[9:13]
    attend_back_kernel(*attention, *outs[:5])

    @pl.when(core_ref[0] == 0)
    def _():
        normed_back_kernel(*norm, *outs[:3], first_here, second_here, first_there, *outs[5:])

    @pl.when(core_ref[0] != 0)
    def _():
        normed_back_kernel(*norm, *outs[:3], first_there, second_there, first_here, *outs[5:])


def front_back_call(core, length, query, key, value, grad, first, hat, inverse, scale, weights):
    like = jax.ShapeDtypeStruct(query.shape, jnp.bfloat16)
    line = jax.ShapeDtypeStruct((1, query.shape[1]), jnp.float32)
    return pl.pallas_call(
        front_back_kernel,
        out_shape=(like, like, like, line, line, like, line, line),
        in_specs=[SMEM, SMEM] + whole(12),
        out_specs=tuple(whole(8)),
        cost_estimate=cost(1),
        name="front_back",
    )(
        core.reshape(1), length, query, key, value, grad,
        first, hat, inverse, scale.reshape(1, -1), *weights,
    )


def finish_hidden_kernel(quarter_ref, own_ref, other_ref, outer_ref, inner_ref):
    rows, width = inner_ref.shape[0], outer_ref.shape[1]
    parts = []
    for q in range(4):
        where = q ^ quarter_ref[0]
        own = own_ref[where // 2].astype(jnp.float32)
        other = other_ref[where // 2].astype(jnp.float32)
        item = jnp.where(where % 2 == 0, own, other)
        outer_ref[q * rows : (q + 1) * rows] = item[:rows]
        parts.append(item[rows:])
    inner_ref[...] = jnp.concatenate(
        [part[:, o * rows : (o + 1) * rows] for o in range(width // rows) for part in parts], axis=1
    )


def finish_hidden_call(quarter, own, other):
    rows, width = own.shape[1] // 2, own.shape[2]
    return pl.pallas_call(
        finish_hidden_kernel,
        out_shape=(
            jax.ShapeDtypeStruct((4 * rows, width), jnp.float32),
            jax.ShapeDtypeStruct((rows, 4 * width), jnp.float32),
        ),
        in_specs=[SMEM] + whole(2),
        out_specs=tuple(whole(2)),
        cost_estimate=cost(1),
        name="finish_hidden",
    )(quarter.reshape(1), own, other)


def finish_late_kernel(place_ref, own_ref, other_ref, *outs):
    core, chip = place_ref[0], place_ref[1]
    rows, place_part = outs[0].shape[0], outs[4].shape[0] // 2
    half, lanes = rows // 2, outs[5].shape[1]
    base = rows + place_part

    def fill(lows, highs):
        for i, source in enumerate((lows, highs)):
            data = source[...].astype(jnp.float32)
            outs[2 * i][...] = data[:rows]
            outs[4][i * place_part : (i + 1) * place_part] = data[rows:base]
            outs[5][8 * i : 8 * i + 8] = data[base : base + 8, :lanes]
            second = outs[2 * i + 1]
            second[pl.ds(pl.multiple_of(chip * half, 8), half)] = data[base + 8 : base + 8 + half]
            second[pl.ds(pl.multiple_of((1 - chip) * half, 8), half)] = data[base + 8 + half :]

    @pl.when(core == 0)
    def _():
        fill(own_ref, other_ref)

    @pl.when(core != 0)
    def _():
        fill(other_ref, own_ref)


def finish_late_call(core, chip, own, other, rows, place_part):
    width = own.shape[1]
    square = jax.ShapeDtypeStruct((rows, width), jnp.float32)
    return pl.pallas_call(
        finish_late_kernel,
        out_shape=(square,) * 4
        + (
            jax.ShapeDtypeStruct((2 * place_part, width), jnp.float32),
            jax.ShapeDtypeStruct((16, 128 * -(-rows // 128)), jnp.float32),
        ),
        in_specs=[SMEM] + whole(2),
        out_specs=tuple(whole(6)),
        cost_estimate=cost(1),
        name="finish_late",
    )(jnp.stack([core, chip]), own, other)


def widen_kernel(core_ref, here_ref, there_ref, out_ref):
    wide = here_ref.shape[1]

    @pl.when(core_ref[0] == 0)
    def _():
        out_ref[:, :wide] = here_ref[...].astype(jnp.float32)
        out_ref[:, wide:] = there_ref[...].astype(jnp.float32)

    @pl.when(core_ref[0] != 0)
    def _():
        out_ref[:, :wide] = there_ref[...].astype(jnp.float32)
        out_ref[:, wide:] = here_ref[...].astype(jnp.float32)


def widen_call(core, here, there):
    count, wide = here.shape
    tile = count // 8
    return pl.pallas_call(
        widen_kernel,
        grid=(8,),
        out_shape=jax.ShapeDtypeStruct((count, 2 * wide), jnp.float32),
        in_specs=[SMEM] + [pl.BlockSpec((tile, wide), lambda i: (i, 0))] * 2,
        out_specs=pl.BlockSpec((tile, 2 * wide), lambda i: (i, 0)),
        cost_estimate=cost(5),
        name="widen",
    )(core.reshape(1), here, there)


def on_device(
    groups,
    owners,
    token_ids,
    lengths,
    word_table,
    position_table,
    embed_gain,
    embed_bias,
    query_weight,
    query_bias,
    key_weight,
    value_weight,
    value_bias,
    output_weight,
    output_bias,
    middle_gain,
    middle_bias,
    inner_weight,
    inner_bias,
    outer_weight,
    outer_bias,
    final_gain,
    final_bias,
    cotangent,
):
    links = Links(groups, owners)
    table_rows, width = word_table.shape
    full_len = token_ids.shape[1]
    rows = query_weight.shape[0]
    hidden = inner_weight.shape[1]
    cap = 2 * full_len // owners
    place_part = position_table.shape[0] // 2
    dp = lax.axis_index("dp")
    core, quarter = dp % 2, dp % 4
    blocks = [quarter, quarter ^ 1, quarter ^ 2, quarter ^ 3]
    ids = token_ids.reshape(full_len)

    inner_quarter = pick(inner_weight.reshape(rows, owners, 4, rows), quarter, 2)
    hidden_piece = jnp.concatenate(
        [
            inner_quarter.reshape(rows, width),
            lax.dynamic_slice_in_dim(outer_weight, quarter * rows, rows, 0),
        ]
    )
    vectors = [
        embed_gain, embed_bias, query_bias, value_bias, output_bias, middle_gain, middle_bias,
        outer_bias, final_gain, final_bias,
    ]
    vectors += [inner_bias[i * rows : (i + 1) * rows] for i in range(4)]
    vector_piece = sum(
        lax.pad(
            item.reshape(1, rows),
            jnp.zeros((), jnp.bfloat16),
            ((i, 15 - i, 0), (0, width - rows, 0)),
        )
        for i, item in enumerate(vectors)
    )
    square_piece = jnp.concatenate(
        [
            jnp.where(core == 0, query_weight, value_weight),
            jnp.where(core == 0, key_weight, output_weight),
            lax.dynamic_slice_in_dim(position_table, core * place_part, place_part, 0),
            vector_piece,
        ]
    )

    owner = ids // table_rows
    local = ids - owner * table_rows
    onehot = owner[:, None] == lax.iota(jnp.int32, owners)[None, :]
    before = lax.iota(jnp.int32, full_len)
    lower = (before[:, None] > before[None, :]).astype(jnp.bfloat16)
    ranks = matmul(lower, onehot.astype(jnp.bfloat16))
    rank = jnp.sum(jnp.where(onehot, ranks, 0.0), axis=1).astype(jnp.int32)
    slot = owner * cap + rank
    slots = lax.iota(jnp.int32, owners * cap)
    sent_ids = jnp.sum(
        jnp.where(slots[:, None] == slot[None, :], local[None, :] + 1, 0), axis=1
    ) - 1
    held_ids = lax.all_to_all(sent_ids.reshape(owners, cap), "vocab", 0, 0, tiled=True).reshape(-1)

    picked = jnp.take(word_table, jnp.maximum(held_ids, 0), axis=0)
    hidden_pieces, square_pieces, beyond_pieces = [], [], []
    hidden_held, square_held = hidden_piece, square_piece
    A = links.A
    for step in range(A):
        square_row, hidden_row = links.row(square_held), links.row(hidden_held)
        square_next, hidden_next = (), ()
        if step < A - 1:
            square_next, hidden_next = links.step_a(square_held), links.step_a(hidden_held)
        crossing = [links.swap(piece, 2) for piece in hidden_pieces[len(beyond_pieces) :]]
        if step == A - 1:
            arrived = lax.all_to_all(
                picked.reshape(owners, cap, width), "vocab", 0, 0, tiled=True
            )
        tied = tie(square_row, square_next, hidden_row, hidden_next, crossing, picked)
        square_row, square_held, hidden_row, hidden_held, crossing, picked = tied
        square_pieces += square_row
        hidden_pieces += hidden_row
        beyond_pieces += crossing
    sources = links.sources()
    first_here, second_here, place_here, small = arrange(
        sources,
        square_pieces,
        [(0, rows), (rows, rows), (2 * rows, place_part), (2 * rows + place_part, 16)],
        [width, width, width, 128 * -(-rows // 128)],
    )
    first_there, second_there, place_there = (
        links.swap(item, 1) for item in (first_here, second_here, place_here)
    )
    beyond_pieces += [links.swap(piece, 2) for piece in hidden_pieces[len(beyond_pieces) :]]
    bands = [(0, rows), (rows, rows)]
    inner_here, outer_here = arrange(sources, hidden_pieces, bands, [width, width])
    inner_beyond, outer_beyond = arrange(sources, beyond_pieces, bands, [width, width])
    arrived, inner_here, outer_here, inner_beyond, outer_beyond = tie(
        arrived, inner_here, outer_here, inner_beyond, outer_beyond
    )

    small = jnp.transpose(small[:, :, :rows], (1, 0, 2)).reshape(16, width).astype(jnp.float32)
    (
        embed_scale, embed_shift, query_shift, value_shift, output_shift, middle_scale,
        middle_shift, outer_shift, final_scale, final_shift,
    ) = (small[i] for i in range(10))
    inner_shift = jnp.stack([pick(small, 10 + i) for i in blocks])

    def ordered(here, there):
        return jnp.where(core == 0, here, there), jnp.where(core == 0, there, here)

    matrices = [
        item.reshape(width, width)
        for item in (first_here, first_there, second_here, second_there)
    ]
    output_matrix = jnp.where(core == 0, matrices[3], matrices[2])
    place_rows = jnp.stack(ordered(place_here, place_there), axis=1).reshape(full_len, width)

    route = (slot[:, None] == slots[None, :]).astype(jnp.bfloat16)
    embedded = matmul(route, arrived.reshape(owners * cap, width))
    summed = embedded + place_rows.astype(jnp.float32)
    normed, hat_embed, inv_embed = normalize(summed, embed_scale, embed_shift)
    normed_low = normed.astype(jnp.bfloat16)
    query_low, key_low, value_low = project_call(
        core, normed_low, matrices, query_shift, value_shift
    )
    inner_beside, outer_beside = links.swap(inner_here, 1), links.swap(outer_here, 1)
    context = attend_call(lengths, query_low, key_low, value_low)
    inner_matrix = [inner_here, inner_beside, inner_beyond, links.swap(inner_beyond, 1)]
    outer_matrix = [outer_here, outer_beside, outer_beyond, links.swap(outer_beyond, 1)]
    inner_matrix = [item.reshape(width, width) for item in inner_matrix]
    outer_matrix = [item.reshape(width, width) for item in outer_matrix]
    attended = matmul(context, output_matrix) + output_shift
    middle, hat_middle, inv_middle = normalize(normed + attended, middle_scale, middle_shift)
    middle_low = middle.astype(jnp.bfloat16)
    activated, slopes, branch = hidden_call(middle_low, inner_shift, inner_matrix, outer_matrix)
    result, hat_final, inv_final = normalize(
        middle + branch + outer_shift, final_scale, final_shift
    )
    output = result.astype(jnp.bfloat16).reshape(1, full_len, width)

    upstream = cotangent.reshape(full_len, width).astype(jnp.float32)
    final_gain_gradient = jnp.sum(upstream * hat_final, axis=0)
    final_bias_gradient = jnp.sum(upstream, axis=0)
    second = normalize_back(upstream, hat_final, inv_final, final_scale)
    branch_grad = second.astype(jnp.bfloat16)
    outer_bias_gradient = jnp.sum(branch_grad.astype(jnp.float32), axis=0)

    def local_terms(left, right):
        return contract_rows(left, right).astype(jnp.bfloat16).reshape(owners, rows, width)

    outer_terms = [None] * 4
    for i in (3, 1, 2, 0):
        outer_terms[i] = local_terms(activated[i], branch_grad)
    outer_cross = [links.swap(outer_terms[i], 1) for i in (3, 1)]
    inner_grad = [
        (times_transposed(branch_grad, outer_matrix[i]) * slopes[i].astype(jnp.float32)).astype(jnp.bfloat16)
        for i in range(4)
    ]
    inner_grad, outer_cross = tie(inner_grad, outer_cross)
    outer_pair = jnp.concatenate(
        [add(outer_terms[0], outer_cross[1]), add(outer_terms[2], outer_cross[0])], axis=1
    )
    outer_pair, inner_grad = tie(links.split(outer_pair, 0), inner_grad)
    inner_bias_gradient = [jnp.sum(item.astype(jnp.float32), axis=0) for item in inner_grad]
    inner_terms = [None] * 4
    for i in (3, 1, 2, 0):
        inner_terms[i] = contract_rows(middle_low, inner_grad[i]).astype(jnp.bfloat16)
        inner_terms[i] = inner_terms[i].reshape(owners, rows, width)
    inner_cross = [links.swap(inner_terms[i], 1) for i in (3, 1)]
    middle_grad = second + sum(times_transposed(inner_grad[i], inner_matrix[i]) for i in range(4))
    middle_grad, inner_cross = tie(middle_grad, inner_cross)
    inner_sent, middle_grad = tie(add(inner_terms[2], inner_cross[0]), middle_grad)
    inner_near = add(inner_terms[0], inner_cross[1])
    middle_gain_gradient = jnp.sum(middle_grad * hat_middle, axis=0)
    middle_bias_gradient = jnp.sum(middle_grad, axis=0)
    first = normalize_back(middle_grad, hat_middle, inv_middle, middle_scale)
    attended_grad = first.astype(jnp.bfloat16)
    output_bias_gradient = jnp.sum(attended_grad.astype(jnp.float32), axis=0)
    context_grad = times_transposed(attended_grad, output_matrix).astype(jnp.bfloat16)
    outer_sent, outer_kept = links.last_b(outer_pair, 0)
    context_grad, inner_sent, outer_sent = tie(context_grad, inner_sent, outer_sent)
    inner_across = links.swap(inner_sent, 2)
    outer_held = links.step_b(outer_sent)
    back = front_back_call(
        core, lengths, query_low, key_low, value_low, context_grad, first, hat_embed, inv_embed,
        embed_scale, matrices,
    )
    back, inner_across, outer_held = tie(back, inner_across, outer_held)
    (
        query_low_grad, key_low_grad, value_low_grad, query_bias_gradient, value_bias_gradient,
        embedded_grad, embed_gain_gradient, embed_bias_gradient,
    ) = back
    own_left = jnp.where(core == 0, normed_low, context)
    sent_left = jnp.where(core == 0, context, normed_low)
    square_sent = [
        local_terms(normed_low, jnp.where(core == 0, value_low_grad, query_low_grad)),
        local_terms(sent_left, jnp.where(core == 0, attended_grad, key_low_grad)),
    ]
    square_own = [
        local_terms(normed_low, jnp.where(core == 0, query_low_grad, value_low_grad)),
        local_terms(own_left, jnp.where(core == 0, key_low_grad, attended_grad)),
    ]
    square_cross = [links.swap(item, 1) for item in square_sent]
    outer_half = add(outer_held, outer_kept)
    outer_across = links.swap(outer_half[:, rows:], 2)
    inner_half = links.fold_b(links.split(add(inner_near, inner_across), 0), 0)
    wide = width // 2
    leaving = jnp.einsum("ts,td->sd", route, embedded_grad, preferred_element_type=jnp.float32)
    leaving = leaving.astype(jnp.bfloat16).reshape(owners, cap, width)
    parts = 2
    cut = cap // parts
    known = jnp.stack(
        [
            item.reshape(owners, parts, cut).transpose(1, 0, 2)
            for item in (held_ids, links.swap(held_ids, 1))
        ],
        axis=1,
    ).reshape(-1)
    known_sets = [known]
    bit = 2
    while bit < groups:
        known_sets += [links.swap(item, bit) for item in known_sets]
        bit *= 2
    sums = [
        embed_gain_gradient, embed_bias_gradient, query_bias_gradient, value_bias_gradient,
        output_bias_gradient, middle_gain_gradient, middle_bias_gradient, outer_bias_gradient,
        final_gain_gradient, final_bias_gradient,
    ]
    inner_bias_gradient = jnp.stack(inner_bias_gradient)[jnp.stack(blocks)]
    vector_terms = jnp.concatenate(
        [item.reshape(1, width) for item in sums] + [inner_bias_gradient]
    )
    vector_terms = vector_terms.reshape(14, owners, rows).transpose(1, 0, 2)
    vector_terms = jnp.pad(vector_terms, ((0, 0), (0, 2), (0, width - rows)))
    vector_terms = vector_terms.reshape(owners, 2, 8, width).astype(jnp.bfloat16)
    place_terms = embedded_grad.reshape(owners, 2, place_part, width)
    late_terms = jnp.concatenate([place_terms, vector_terms], axis=2)
    late_cross = links.swap(pick(late_terms, 1 - core, 1), 1)
    bits = []
    bit = 2
    while bit < groups:
        bits.append(bit)
        bit *= 2

    def exchange(part):
        piece = leaving[:, part * cut : (part + 1) * cut]
        return lax.all_to_all(piece, "vocab", 0, 0, tiled=True)

    def beyond(landed):
        landed = landed.reshape(-1, width)
        mine, theirs = ordered(landed[:, :wide], landed[:, wide:])
        items = [jnp.concatenate([mine, links.swap(theirs, 1)])]
        for bit in bits:
            items = items + [links.swap(item, bit) for item in items]
        return items

    def table_term(pieces, known):
        return matmul((table_ids[:, None] == known[None, :]).astype(jnp.bfloat16), pieces)

    table_ids = lax.iota(jnp.int32, table_rows)
    late_whole = jnp.concatenate(
        [add(square_own[0], square_cross[0]), add(pick(late_terms, core, 1), late_cross)], axis=1
    )
    chip, second_part = dp // 2 % 2, rows // 2
    second_cut = add(square_own[1], square_cross[1]).reshape(owners, 2, second_part, width)
    second_kept, second_sent = pick(second_cut, chip, 1), pick(second_cut, 1 - chip, 1)
    landed, late_whole, leaving, outer_across, inner_half, second_kept, second_sent = tie(
        exchange(0), links.split(late_whole, 0), leaving, outer_across, inner_half, second_kept,
        second_sent,
    )
    second_across = links.swap(second_sent, 2)
    late_half = links.fold_b(late_whole, 0)
    first_sets = beyond(landed)
    outer_cut = links.cut_a(add(outer_half[:, :rows], outer_across), 0)
    outer_arrived = links.sent_a(outer_cut)
    landed, first_sets, outer_arrived, second_across = tie(
        exchange(1), first_sets, outer_arrived, second_across
    )
    second_half = links.fold_b(links.split(add(second_kept, second_across), 0), 0)
    inner_cut = links.cut_a(inner_half, 0)
    inner_arrived = links.sent_a(inner_cut)
    second_sets = beyond(landed)
    table_sum = [table_term(jnp.concatenate([first_sets[0], second_sets[0]]), known_sets[0])]
    table_sum, late_half, second_half, second_sets, inner_arrived = tie(
        table_sum, late_half, second_half, second_sets, inner_arrived
    )
    late_cut = links.cut_a(jnp.concatenate([late_half, second_half], axis=1), 0)
    late_arrived = links.sent_a(late_cut)
    hidden_share = jnp.concatenate(
        [add(outer_cut[0], *outer_arrived), add(inner_cut[0], *inner_arrived)]
    )
    hidden_share = links.far(hidden_share, 4)
    hidden_beyond = links.swap(hidden_share, 2)
    for i in range(1, len(known_sets)):
        pieces = jnp.concatenate([first_sets[i], second_sets[i]])
        table_sum.append(table_term(pieces, known_sets[i]))
    while len(table_sum) > 1:
        table_sum = [a + b for a, b in zip(table_sum[::2], table_sum[1::2])]
    table_half, hidden_beyond, late_arrived = tie(
        table_sum[0].astype(jnp.bfloat16), hidden_beyond, late_arrived
    )
    late_share = add(late_cut[0], *late_arrived)
    hidden_core = jnp.stack([hidden_share, hidden_beyond])
    hidden_other = links.swap(hidden_core, 1)
    table_other = links.swap(table_half, 1)
    late_main = links.far(late_share[: late_share.shape[0] - second_part], 2)
    late_second = links.far(late_share[late_share.shape[0] - second_part :], 4)
    late_core = jnp.concatenate([late_main, late_second, links.swap(late_second, 2)])
    late_other = links.swap(late_core, 1)
    outer_weight_gradient, inner_weight_gradient = finish_hidden_call(
        quarter, hidden_core, hidden_other
    )
    first_share, second_share, third_share, fourth_share, position_gradient, vector_share = (
        finish_late_call(core, chip, late_core, late_other, rows, place_part)
    )
    vector_share = vector_share[:, :rows]
    table_gradient = widen_call(core, table_half, table_other)
    (
        embed_gain_gradient, embed_bias_gradient, query_bias_gradient, value_bias_gradient,
        output_bias_gradient, middle_gain_gradient, middle_bias_gradient, outer_bias_gradient,
        final_gain_gradient, final_bias_gradient,
    ) = (vector_share[i] for i in range(10))
    inner_bias_gradient = vector_share[10:14].reshape(4 * rows)

    return (
        output,
        table_gradient,
        position_gradient,
        embed_gain_gradient,
        embed_bias_gradient,
        first_share,
        query_bias_gradient,
        second_share,
        third_share,
        value_bias_gradient,
        fourth_share,
        output_bias_gradient,
        middle_gain_gradient,
        middle_bias_gradient,
        inner_weight_gradient,
        inner_bias_gradient,
        outer_weight_gradient,
        outer_bias_gradient,
        final_gain_gradient,
        final_bias_gradient,
    )


def solution(mesh):
    return jax.shard_map(
        functools.partial(on_device, mesh.shape["dp"], mesh.shape["vocab"]),
        mesh=mesh,
        in_specs=(
            P(("dp", "vocab"), None),
            P(("dp", "vocab")),
            P("vocab", None),
            P("vocab", None),
            P("vocab"),
            P("vocab"),
            P("vocab", None),
            P("vocab"),
            P("vocab", None),
            P("vocab", None),
            P("vocab"),
            P("vocab", None),
            P("vocab"),
            P("vocab"),
            P("vocab"),
            P("vocab", None),
            P("vocab"),
            P("vocab", None),
            P("vocab"),
            P("vocab"),
            P("vocab"),
            P(("dp", "vocab"), None, None),
        ),
        out_specs=(
            P(("dp", "vocab"), None, None),
            P("vocab", None),
            P("vocab", None),
            P("vocab"),
            P("vocab"),
            P("vocab", None),
            P("vocab"),
            P("vocab", None),
            P("vocab", None),
            P("vocab"),
            P("vocab", None),
            P("vocab"),
            P("vocab"),
            P("vocab"),
            P("vocab", None),
            P("vocab"),
            P("vocab", None),
            P("vocab"),
            P("vocab"),
            P("vocab"),
        ),
        check_vma=False,
    )
```

```python
import functools
import math

import jax
import jax.numpy as jnp
from jax import lax
from jax.experimental import pallas as pl
from jax.experimental.pallas import tpu as pltpu
from jax.sharding import PartitionSpec as P

HEADS = 12


epsilon = 1e-12
scaling = 0.125


def normalize(values, gain, bias_row):
    center = values - jnp.mean(values, axis=-1, keepdims=True)
    inverse = lax.rsqrt(jnp.mean(center * center, axis=-1, keepdims=True) + epsilon)
    scaled = center * inverse
    return (scaled * gain + bias_row, scaled, inverse)


def normalize_back(upstream, scaled, inverse, gain):
    weighted = upstream * gain
    return inverse * (
        weighted
        - jnp.mean(weighted, axis=-1, keepdims=True)
        - scaled * jnp.mean(weighted * scaled, axis=-1, keepdims=True)
    )


def gelu_slope(inner):
    cumulative = 0.5 * (1.0 + lax.erf(inner * (1.0 / math.sqrt(2.0))))
    density = jnp.exp(-0.5 * inner * inner) * (1.0 / math.sqrt(2.0 * math.pi))
    return cumulative + inner * density


def matmul(left, right):
    return jnp.dot(left, right, preferred_element_type=jnp.float32)


def contract_rows(left, right):
    return jnp.einsum("ti,tj->ij", left, right, preferred_element_type=jnp.float32)


def times_transposed(left, right):
    return jnp.einsum("tj,ij->ti", left, right, preferred_element_type=jnp.float32)


def split_heads(rows):
    return rows.reshape(rows.shape[0], HEADS, rows.shape[1] // HEADS)


def masked_scores(query_heads, key_heads, visible):
    scores = (
        jnp.einsum("qhd,khd->hqk", query_heads, key_heads, preferred_element_type=jnp.float32)
        * scaling
    )
    return jnp.where(visible[None, None, :], scores, -1e30)


def attend(inputs):
    query_rows, key_rows, value_rows, visible = inputs
    query_heads = split_heads(query_rows)
    scores = masked_scores(query_heads, split_heads(key_rows), visible)
    largest = jnp.max(scores, axis=-1, keepdims=True)
    raised = jnp.exp(scores - largest)
    totals = jnp.sum(raised, axis=-1, keepdims=True)
    probs = raised / totals
    context = jnp.einsum(
        "hqk,khd->qhd",
        probs.astype(jnp.bfloat16),
        split_heads(value_rows),
        preferred_element_type=jnp.float32,
    )
    return (context.reshape(query_rows.shape).astype(jnp.bfloat16), largest + jnp.log(totals))


def attend_back(inputs):
    query_rows, key_rows, value_rows, visible, kept_lse, context_grad = inputs
    query_heads = split_heads(query_rows)
    key_heads = split_heads(key_rows)
    value_heads = split_heads(value_rows)
    grad_heads = split_heads(context_grad)
    probs = jnp.exp(masked_scores(query_heads, key_heads, visible) - kept_lse)
    prob_grad = jnp.einsum(
        "qhd,khd->hqk", grad_heads, value_heads, preferred_element_type=jnp.float32
    )
    centered = prob_grad - jnp.sum(prob_grad * probs, axis=-1, keepdims=True)
    score_grad = (probs * centered).astype(jnp.bfloat16)
    query_grad = (
        jnp.einsum("hqk,khd->qhd", score_grad, key_heads, preferred_element_type=jnp.float32)
        * scaling
    )
    key_grad = (
        jnp.einsum("hqk,qhd->khd", score_grad, query_heads, preferred_element_type=jnp.float32)
        * scaling
    )
    value_grad = jnp.einsum(
        "hqk,qhd->khd", probs.astype(jnp.bfloat16), grad_heads, preferred_element_type=jnp.float32
    )
    return (
        query_grad.reshape(query_rows.shape),
        key_grad.reshape(key_rows.shape),
        value_grad.reshape(value_rows.shape),
    )


class Links:
    def __init__(self, groups, owners):
        self.groups, self.owners = groups, owners
        self.A = 4 if owners % 4 == 0 else 1
        self.B = owners // self.A

    def place(self):
        vocab = lax.axis_index("vocab")
        return vocab // self.B, vocab % self.B

    def step_a(self, piece, far=1):
        A, B = self.A, self.B
        pairs = [(a * B + b, (a + far) % A * B + b) for a in range(A) for b in range(B)]
        return lax.ppermute(piece, "vocab", pairs)

    def step_b(self, piece):
        A, B = self.A, self.B
        pairs = [(a * B + b, a * B + (b + 1) % B) for a in range(A) for b in range(B)]
        return lax.ppermute(piece, "vocab", pairs)

    def swap(self, piece, bit):
        return lax.ppermute(piece, "dp", [(i, i ^ bit) for i in range(self.groups)])

    def row(self, piece):
        pieces = [piece]
        for _ in range(1, self.B):
            pieces.append(self.step_b(pieces[-1]))
        return pieces

    def sources(self):
        a, b = self.place()
        A, B = self.A, self.B
        return jnp.stack([(a - k + A) % A * B + (b - m + B) % B for k in range(A) for m in range(B)])

    def fold_b(self, total, axis):
        sent, kept = self.last_b(total, axis)
        return add(self.step_b(sent), kept)

    def last_b(self, total, axis):
        B = self.B
        here = self.place()[1]

        def block(index):
            return pick(total, index % B, axis + 1)

        held = block(here - 1 + B)
        for s in range(1, B - 1):
            held = add(self.step_b(held), block(here - 1 - s + 2 * B))
        return held, block(here)

    def cut_a(self, total, axis):
        here = self.place()[0]
        return [pick(total, (here + far) % self.A, axis) for far in range(self.A)]

    def sent_a(self, terms):
        return [self.step_a(terms[far], far) for far in range(1, self.A)]

    def split(self, total, axis):
        return total.reshape(total.shape[:axis] + (self.A, self.B) + total.shape[axis + 1 :])

    def far(self, piece, first):
        bit = first
        while bit < self.groups:
            piece = add(piece, self.swap(piece, bit))
            bit *= 2
        return piece


def add(*terms):
    return sum(term.astype(jnp.float32) for term in terms).astype(jnp.bfloat16)


def tie(*values):
    return lax.optimization_barrier(values)


def gelu(inner):
    return inner * (0.5 * (1.0 + lax.erf(inner * (1.0 / math.sqrt(2.0)))))


def pick(stacked, index, axis=0):
    return lax.dynamic_index_in_dim(stacked, index, axis, keepdims=False)


def arrange(sources, pieces, bands, lanes):
    owners = len(pieces)

    def body(sources_ref, *refs):
        ins, outs = refs[:owners], refs[owners:]
        for i in range(owners):
            where = sources_ref[i]
            for (start, size), wide, out in zip(bands, lanes, outs):
                out[where] = ins[i][start : start + size, :wide]

    return pl.pallas_call(
        body,
        out_shape=tuple(
            jax.ShapeDtypeStruct((owners, size, wide), pieces[0].dtype)
            for (start, size), wide in zip(bands, lanes)
        ),
        in_specs=[pl.BlockSpec(memory_space=pltpu.SMEM)]
        + [pl.BlockSpec(memory_space=pltpu.VMEM)] * owners,
        out_specs=tuple(pl.BlockSpec(memory_space=pltpu.VMEM) for _ in bands),
        cost_estimate=pl.CostEstimate(
            flops=0, bytes_accessed=4 * owners * pieces[0].size, transcendentals=0
        ),
        name="arrange",
    )(sources, *pieces)


def cost(micros):
    return pl.CostEstimate(flops=0, bytes_accessed=int(micros * 3e6), transcendentals=0)


def whole(count):
    return [pl.BlockSpec(memory_space=pltpu.VMEM)] * count


SMEM = pl.BlockSpec(memory_space=pltpu.SMEM)


def dot(left, right, dims=((1,), (0,))):
    return lax.dot_general(left, right, (dims, ((), ())), preferred_element_type=jnp.float32)


def head_masks(shape):
    low = lax.broadcasted_iota(jnp.int32, shape, 1) < shape[1] // 2
    return low, jnp.logical_not(low)


def project_kernel(
    core_ref, rows_ref, first_here, first_there, second_here, second_there, query_shift, value_shift,
    query_ref, key_ref, value_ref,
):
    rows = rows_ref[...]

    def fill(query, key, value):
        query_ref[...] = (dot(rows, query[...]) + query_shift[...]).astype(jnp.bfloat16)
        key_ref[...] = dot(rows, key[...]).astype(jnp.bfloat16)
        value_ref[...] = (dot(rows, value[...]) + value_shift[...]).astype(jnp.bfloat16)

    @pl.when(core_ref[0] == 0)
    def _():
        fill(first_here, second_here, first_there)

    @pl.when(core_ref[0] != 0)
    def _():
        fill(first_there, second_there, first_here)


def project_call(core, rows, matrices, query_shift, value_shift):
    like = jax.ShapeDtypeStruct(rows.shape, jnp.bfloat16)
    return pl.pallas_call(
        project_kernel,
        out_shape=(like, like, like),
        in_specs=[SMEM] + whole(7),
        out_specs=tuple(whole(3)),
        cost_estimate=cost(4),
        name="project",
    )(core.reshape(1), rows, *matrices, query_shift.reshape(1, -1), value_shift.reshape(1, -1))


def attend_kernel(length_ref, query_ref, key_ref, value_ref, context_ref):
    count, wide = query_ref.shape[0], 2 * query_ref.shape[1] // HEADS
    hidden_keys = lax.broadcasted_iota(jnp.int32, (count, count), 1) >= length_ref[0]

    @pl.loop(0, HEADS // 2)
    def _(pair):
        lanes = pl.ds(pl.multiple_of(pair * wide, wide), wide)
        query, key, value = query_ref[:, lanes], key_ref[:, lanes], value_ref[:, lanes]
        query = query * scaling
        masks = head_masks((count, wide))
        parts = []
        for mask in masks:
            scores = dot(jnp.where(mask, query, 0).astype(jnp.bfloat16), key, ((1,), (1,)))
            scores = jnp.where(hidden_keys, -1e30, scores)
            raised = jnp.exp(scores - jnp.max(scores, axis=1, keepdims=True))
            totals = jnp.sum(raised, axis=1, keepdims=True)
            parts.append(dot(raised.astype(jnp.bfloat16), value) / totals)
        context_ref[:, lanes] = jnp.where(masks[0], parts[0], parts[1]).astype(jnp.bfloat16)


def attend_call(length, query, key, value):
    return pl.pallas_call(
        attend_kernel,
        out_shape=jax.ShapeDtypeStruct(query.shape, jnp.bfloat16),
        in_specs=[SMEM] + whole(3),
        out_specs=pl.BlockSpec(memory_space=pltpu.VMEM),
        cost_estimate=cost(4),
        name="attend",
    )(length, query, key, value)


def attend_back_kernel(
    length_ref, query_ref, key_ref, value_ref, grad_ref,
    query_grad_ref, key_grad_ref, value_grad_ref, query_sum_ref, value_sum_ref,
):
    count, wide = query_ref.shape[0], 2 * query_ref.shape[1] // HEADS
    half = wide // 2
    hidden_keys = lax.broadcasted_iota(jnp.int32, (count, count), 0) >= length_ref[0]

    @pl.loop(0, HEADS // 2)
    def _(pair):
        lanes = pl.ds(pl.multiple_of(pair * wide, wide), wide)
        query, key = query_ref[:, lanes] * scaling, key_ref[:, lanes]
        query = query.astype(jnp.bfloat16)
        value, grad = value_ref[:, lanes], grad_ref[:, lanes]
        across = jnp.transpose(key.astype(jnp.float32)).astype(jnp.bfloat16)
        masks = head_masks((count, wide))
        query_parts, key_parts, value_parts = [], [], []
        for i, mask in enumerate(masks):
            scores = dot(key, jnp.where(mask, query, 0).astype(jnp.bfloat16), ((1,), (1,)))
            scores = jnp.where(hidden_keys, -1e30, scores)
            raised = jnp.exp(scores - jnp.max(scores, axis=0, keepdims=True))
            probs = raised * (1.0 / jnp.sum(raised, axis=0, keepdims=True))
            prob_grad = dot(jnp.where(mask, value, 0).astype(jnp.bfloat16), grad, ((1,), (1,)))
            centered = prob_grad - jnp.sum(prob_grad * probs, axis=0, keepdims=True)
            score_grad = (probs * centered).astype(jnp.bfloat16)
            value_parts.append(dot(probs.astype(jnp.bfloat16), grad))
            key_parts.append(dot(score_grad, query))
            query_parts.append(dot(across[i * half : (i + 1) * half], score_grad))
        value_grad = jnp.where(masks[0], value_parts[0], value_parts[1]).astype(jnp.bfloat16)
        value_grad_ref[:, lanes] = value_grad
        value_sum_ref[:, lanes] = jnp.sum(value_grad.astype(jnp.float32), axis=0, keepdims=True)
        key_grad = jnp.where(masks[0], key_parts[0], key_parts[1])
        key_grad_ref[:, lanes] = key_grad.astype(jnp.bfloat16)
        query_grad = jnp.transpose(jnp.concatenate(query_parts, axis=0) * scaling)
        query_grad = query_grad.astype(jnp.bfloat16)
        query_grad_ref[:, lanes] = query_grad
        query_sum_ref[:, lanes] = jnp.sum(query_grad.astype(jnp.float32), axis=0, keepdims=True)


def hidden_kernel(rows_ref, shift_ref, *refs):
    inner_refs, outer_refs, active_refs, slope_refs = (refs[4 * i : 4 * i + 4] for i in range(4))
    branch_ref = refs[16]
    width = rows_ref.shape[1]
    tile = 256
    branch_ref[...] = jnp.zeros_like(branch_ref)
    for i in range(4):

        @pl.loop(0, width // tile)
        def _(part, i=i):
            lanes = pl.ds(pl.multiple_of(part * tile, tile), tile)
            inner = dot(rows_ref[...], inner_refs[i][:, lanes]) + shift_ref[i : i + 1, lanes]
            cumulative = 0.5 * (1.0 + lax.erf(inner * (1.0 / math.sqrt(2.0))))
            density = jnp.exp(-0.5 * inner * inner) * (1.0 / math.sqrt(2.0 * math.pi))
            active = (inner * cumulative).astype(jnp.bfloat16)
            active_refs[i][:, lanes] = active
            slope_refs[i][:, lanes] = (cumulative + inner * density).astype(jnp.bfloat16)
            branch_ref[...] += dot(active, outer_refs[i][lanes, :])


def hidden_call(rows, shift, inner, outer):
    like = jax.ShapeDtypeStruct(rows.shape, jnp.bfloat16)
    out = pl.pallas_call(
        hidden_kernel,
        out_shape=(like,) * 8 + (jax.ShapeDtypeStruct(rows.shape, jnp.float32),),
        in_specs=whole(10),
        out_specs=tuple(whole(9)),
        cost_estimate=cost(8),
        name="hidden",
    )(rows, shift, *inner, *outer)
    return out[:4], out[4:8], out[8]


def normed_back_kernel(first_ref, hat_ref, inverse_ref, scale_ref, *refs):
    grads, weights, (out_ref, gain_ref, bias_ref) = refs[:3], refs[3:6], refs[6:]
    upstream = first_ref[...]
    for grad, weight in zip(grads, weights):
        upstream = upstream + dot(grad[...], weight[...], ((1,), (1,)))
    hat = hat_ref[...]
    gain_ref[...] = jnp.sum(upstream * hat, axis=0, keepdims=True)
    bias_ref[...] = jnp.sum(upstream, axis=0, keepdims=True)
    out_ref[...] = normalize_back(upstream, hat, inverse_ref[...], scale_ref[...]).astype(jnp.bfloat16)


def front_back_kernel(*refs):
    core_ref, refs = refs[0], refs[1:]
    attention, norm, outs = refs[:5], refs[5:9], refs[13:]
    first_here, first_there, second_here, second_there = refs[9:13]
    attend_back_kernel(*attention, *outs[:5])

    @pl.when(core_ref[0] == 0)
    def _():
        normed_back_kernel(*norm, *outs[:3], first_here, second_here, first_there, *outs[5:])

    @pl.when(core_ref[0] != 0)
    def _():
        normed_back_kernel(*norm, *outs[:3], first_there, second_there, first_here, *outs[5:])


def front_back_call(core, length, query, key, value, grad, first, hat, inverse, scale, weights):
    like = jax.ShapeDtypeStruct(query.shape, jnp.bfloat16)
    line = jax.ShapeDtypeStruct((1, query.shape[1]), jnp.float32)
    return pl.pallas_call(
        front_back_kernel,
        out_shape=(like, like, like, line, line, like, line, line),
        in_specs=[SMEM, SMEM] + whole(12),
        out_specs=tuple(whole(8)),
        cost_estimate=cost(1),
        name="front_back",
    )(
        core.reshape(1), length, query, key, value, grad,
        first, hat, inverse, scale.reshape(1, -1), *weights,
    )


def finish_hidden_kernel(quarter_ref, own_ref, other_ref, outer_ref, inner_ref):
    rows, width = inner_ref.shape[0], outer_ref.shape[1]
    parts = []
    for q in range(4):
        where = q ^ quarter_ref[0]
        own = own_ref[where // 2].astype(jnp.float32)
        other = other_ref[where // 2].astype(jnp.float32)
        item = jnp.where(where % 2 == 0, own, other)
        outer_ref[q * rows : (q + 1) * rows] = item[:rows]
        parts.append(item[rows:])
    inner_ref[...] = jnp.concatenate(
        [part[:, o * rows : (o + 1) * rows] for o in range(width // rows) for part in parts], axis=1
    )


def finish_hidden_call(quarter, own, other):
    rows, width = own.shape[1] // 2, own.shape[2]
    return pl.pallas_call(
        finish_hidden_kernel,
        out_shape=(
            jax.ShapeDtypeStruct((4 * rows, width), jnp.float32),
            jax.ShapeDtypeStruct((rows, 4 * width), jnp.float32),
        ),
        in_specs=[SMEM] + whole(2),
        out_specs=tuple(whole(2)),
        cost_estimate=cost(1),
        name="finish_hidden",
    )(quarter.reshape(1), own, other)


def finish_late_kernel(place_ref, own_ref, other_ref, *outs):
    core, chip = place_ref[0], place_ref[1]
    rows, place_part = outs[0].shape[0], outs[4].shape[0] // 2
    half, lanes = rows // 2, outs[5].shape[1]
    base = rows + place_part

    def fill(lows, highs):
        for i, source in enumerate((lows, highs)):
            data = source[...].astype(jnp.float32)
            outs[2 * i][...] = data[:rows]
            outs[4][i * place_part : (i + 1) * place_part] = data[rows:base]
            outs[5][8 * i : 8 * i + 8] = data[base : base + 8, :lanes]
            second = outs[2 * i + 1]
            second[pl.ds(pl.multiple_of(chip * half, 8), half)] = data[base + 8 : base + 8 + half]
            second[pl.ds(pl.multiple_of((1 - chip) * half, 8), half)] = data[base + 8 + half :]

    @pl.when(core == 0)
    def _():
        fill(own_ref, other_ref)

    @pl.when(core != 0)
    def _():
        fill(other_ref, own_ref)


def finish_late_call(core, chip, own, other, rows, place_part):
    width = own.shape[1]
    square = jax.ShapeDtypeStruct((rows, width), jnp.float32)
    return pl.pallas_call(
        finish_late_kernel,
        out_shape=(square,) * 4
        + (
            jax.ShapeDtypeStruct((2 * place_part, width), jnp.float32),
            jax.ShapeDtypeStruct((16, 128 * -(-rows // 128)), jnp.float32),
        ),
        in_specs=[SMEM] + whole(2),
        out_specs=tuple(whole(6)),
        cost_estimate=cost(1),
        name="finish_late",
    )(jnp.stack([core, chip]), own, other)


def widen_kernel(core_ref, here_ref, there_ref, out_ref):
    wide = here_ref.shape[1]

    @pl.when(core_ref[0] == 0)
    def _():
        out_ref[:, :wide] = here_ref[...].astype(jnp.float32)
        out_ref[:, wide:] = there_ref[...].astype(jnp.float32)

    @pl.when(core_ref[0] != 0)
    def _():
        out_ref[:, :wide] = there_ref[...].astype(jnp.float32)
        out_ref[:, wide:] = here_ref[...].astype(jnp.float32)


def widen_call(core, here, there):
    count, wide = here.shape
    tile = count // 8
    return pl.pallas_call(
        widen_kernel,
        grid=(8,),
        out_shape=jax.ShapeDtypeStruct((count, 2 * wide), jnp.float32),
        in_specs=[SMEM] + [pl.BlockSpec((tile, wide), lambda i: (i, 0))] * 2,
        out_specs=pl.BlockSpec((tile, 2 * wide), lambda i: (i, 0)),
        cost_estimate=cost(5),
        name="widen",
    )(core.reshape(1), here, there)


def on_device(
    groups,
    owners,
    token_ids,
    lengths,
    word_table,
    position_table,
    embed_gain,
    embed_bias,
    query_weight,
    query_bias,
    key_weight,
    value_weight,
    value_bias,
    output_weight,
    output_bias,
    middle_gain,
    middle_bias,
    inner_weight,
    inner_bias,
    outer_weight,
    outer_bias,
    final_gain,
    final_bias,
    cotangent,
):
    links = Links(groups, owners)
    table_rows, width = word_table.shape
    full_len = token_ids.shape[1]
    rows = query_weight.shape[0]
    hidden = inner_weight.shape[1]
    cap = 2 * full_len // owners
    place_part = position_table.shape[0] // 2
    dp = lax.axis_index("dp")
    core, quarter = dp % 2, dp % 4
    blocks = [quarter, quarter ^ 1, quarter ^ 2, quarter ^ 3]
    ids = token_ids.reshape(full_len)

    inner_quarter = pick(inner_weight.reshape(rows, owners, 4, rows), quarter, 2)
    hidden_piece = jnp.concatenate(
        [
            inner_quarter.reshape(rows, width),
            lax.dynamic_slice_in_dim(outer_weight, quarter * rows, rows, 0),
        ]
    )
    vectors = [
        embed_gain, embed_bias, query_bias, value_bias, output_bias, middle_gain, middle_bias,
        outer_bias, final_gain, final_bias,
    ]
    vectors += [inner_bias[i * rows : (i + 1) * rows] for i in range(4)]
    vector_piece = sum(
        lax.pad(
            item.reshape(1, rows),
            jnp.zeros((), jnp.bfloat16),
            ((i, 15 - i, 0), (0, width - rows, 0)),
        )
        for i, item in enumerate(vectors)
    )
    square_piece = jnp.concatenate(
        [
            jnp.where(core == 0, query_weight, value_weight),
            jnp.where(core == 0, key_weight, output_weight),
            lax.dynamic_slice_in_dim(position_table, core * place_part, place_part, 0),
            vector_piece,
        ]
    )

    owner = ids // table_rows
    local = ids - owner * table_rows
    onehot = owner[:, None] == lax.iota(jnp.int32, owners)[None, :]
    before = lax.iota(jnp.int32, full_len)
    lower = (before[:, None] > before[None, :]).astype(jnp.bfloat16)
    ranks = matmul(lower, onehot.astype(jnp.bfloat16))
    rank = jnp.sum(jnp.where(onehot, ranks, 0.0), axis=1).astype(jnp.int32)
    slot = owner * cap + rank
    slots = lax.iota(jnp.int32, owners * cap)
    sent_ids = jnp.sum(
        jnp.where(slots[:, None] == slot[None, :], local[None, :] + 1, 0), axis=1
    ) - 1
    held_ids = lax.all_to_all(sent_ids.reshape(owners, cap), "vocab", 0, 0, tiled=True).reshape(-1)

    picked = jnp.take(word_table, jnp.maximum(held_ids, 0), axis=0)
    hidden_pieces, square_pieces, beyond_pieces = [], [], []
    hidden_held, square_held = hidden_piece, square_piece
    A = links.A
    for step in range(A):
        square_row, hidden_row = links.row(square_held), links.row(hidden_held)
        square_next, hidden_next = (), ()
        if step < A - 1:
            square_next, hidden_next = links.step_a(square_held), links.step_a(hidden_held)
        crossing = [links.swap(piece, 2) for piece in hidden_pieces[len(beyond_pieces) :]]
        if step == A - 1:
            arrived = lax.all_to_all(
                picked.reshape(owners, cap, width), "vocab", 0, 0, tiled=True
            )
        tied = tie(square_row, square_next, hidden_row, hidden_next, crossing, picked)
        square_row, square_held, hidden_row, hidden_held, crossing, picked = tied
        square_pieces += square_row
        hidden_pieces += hidden_row
        beyond_pieces += crossing
    sources = links.sources()
    first_here, second_here, place_here, small = arrange(
        sources,
        square_pieces,
        [(0, rows), (rows, rows), (2 * rows, place_part), (2 * rows + place_part, 16)],
        [width, width, width, 128 * -(-rows // 128)],
    )
    first_there, second_there, place_there = (
        links.swap(item, 1) for item in (first_here, second_here, place_here)
    )
    beyond_pieces += [links.swap(piece, 2) for piece in hidden_pieces[len(beyond_pieces) :]]
    bands = [(0, rows), (rows, rows)]
    inner_here, outer_here = arrange(sources, hidden_pieces, bands, [width, width])
    inner_beyond, outer_beyond = arrange(sources, beyond_pieces, bands, [width, width])
    arrived, inner_here, outer_here, inner_beyond, outer_beyond = tie(
        arrived, inner_here, outer_here, inner_beyond, outer_beyond
    )

    small = jnp.transpose(small[:, :, :rows], (1, 0, 2)).reshape(16, width).astype(jnp.float32)
    (
        embed_scale, embed_shift, query_shift, value_shift, output_shift, middle_scale,
        middle_shift, outer_shift, final_scale, final_shift,
    ) = (small[i] for i in range(10))
    inner_shift = jnp.stack([pick(small, 10 + i) for i in blocks])

    def ordered(here, there):
        return jnp.where(core == 0, here, there), jnp.where(core == 0, there, here)

    matrices = [
        item.reshape(width, width)
        for item in (first_here, first_there, second_here, second_there)
    ]
    output_matrix = jnp.where(core == 0, matrices[3], matrices[2])
    place_rows = jnp.stack(ordered(place_here, place_there), axis=1).reshape(full_len, width)

    route = (slot[:, None] == slots[None, :]).astype(jnp.bfloat16)
    embedded = matmul(route, arrived.reshape(owners * cap, width))
    summed = embedded + place_rows.astype(jnp.float32)
    normed, hat_embed, inv_embed = normalize(summed, embed_scale, embed_shift)
    normed_low = normed.astype(jnp.bfloat16)
    query_low, key_low, value_low = project_call(
        core, normed_low, matrices, query_shift, value_shift
    )
    inner_beside, outer_beside = links.swap(inner_here, 1), links.swap(outer_here, 1)
    context = attend_call(lengths, query_low, key_low, value_low)
    inner_matrix = [inner_here, inner_beside, inner_beyond, links.swap(inner_beyond, 1)]
    outer_matrix = [outer_here, outer_beside, outer_beyond, links.swap(outer_beyond, 1)]
    inner_matrix = [item.reshape(width, width) for item in inner_matrix]
    outer_matrix = [item.reshape(width, width) for item in outer_matrix]
    attended = matmul(context, output_matrix) + output_shift
    middle, hat_middle, inv_middle = normalize(normed + attended, middle_scale, middle_shift)
    middle_low = middle.astype(jnp.bfloat16)
    activated, slopes, branch = hidden_call(middle_low, inner_shift, inner_matrix, outer_matrix)
    result, hat_final, inv_final = normalize(
        middle + branch + outer_shift, final_scale, final_shift
    )
    output = result.astype(jnp.bfloat16).reshape(1, full_len, width)

    upstream = cotangent.reshape(full_len, width).astype(jnp.float32)
    final_gain_gradient = jnp.sum(upstream * hat_final, axis=0)
    final_bias_gradient = jnp.sum(upstream, axis=0)
    second = normalize_back(upstream, hat_final, inv_final, final_scale)
    branch_grad = second.astype(jnp.bfloat16)
    outer_bias_gradient = jnp.sum(branch_grad.astype(jnp.float32), axis=0)

    def local_terms(left, right):
        return contract_rows(left, right).astype(jnp.bfloat16).reshape(owners, rows, width)

    outer_terms = [None] * 4
    for i in (3, 1, 2, 0):
        outer_terms[i] = local_terms(activated[i], branch_grad)
    outer_cross = [links.swap(outer_terms[i], 1) for i in (3, 1)]
    inner_grad = [
        (times_transposed(branch_grad, outer_matrix[i]) * slopes[i].astype(jnp.float32)).astype(jnp.bfloat16)
        for i in range(4)
    ]
    inner_grad, outer_cross = tie(inner_grad, outer_cross)
    outer_pair = jnp.concatenate(
        [add(outer_terms[0], outer_cross[1]), add(outer_terms[2], outer_cross[0])], axis=1
    )
    outer_pair, inner_grad = tie(links.split(outer_pair, 0), inner_grad)
    inner_bias_gradient = [jnp.sum(item.astype(jnp.float32), axis=0) for item in inner_grad]
    inner_terms = [None] * 4
    for i in (3, 1, 2, 0):
        inner_terms[i] = contract_rows(middle_low, inner_grad[i]).astype(jnp.bfloat16)
        inner_terms[i] = inner_terms[i].reshape(owners, rows, width)
    inner_cross = [links.swap(inner_terms[i], 1) for i in (3, 1)]
    middle_grad = second + sum(times_transposed(inner_grad[i], inner_matrix[i]) for i in range(4))
    middle_grad, inner_cross = tie(middle_grad, inner_cross)
    inner_sent, middle_grad = tie(add(inner_terms[2], inner_cross[0]), middle_grad)
    inner_near = add(inner_terms[0], inner_cross[1])
    middle_gain_gradient = jnp.sum(middle_grad * hat_middle, axis=0)
    middle_bias_gradient = jnp.sum(middle_grad, axis=0)
    first = normalize_back(middle_grad, hat_middle, inv_middle, middle_scale)
    attended_grad = first.astype(jnp.bfloat16)
    output_bias_gradient = jnp.sum(attended_grad.astype(jnp.float32), axis=0)
    context_grad = times_transposed(attended_grad, output_matrix).astype(jnp.bfloat16)
    outer_sent, outer_kept = links.last_b(outer_pair, 0)
    context_grad, inner_sent, outer_sent = tie(context_grad, inner_sent, outer_sent)
    inner_across = links.swap(inner_sent, 2)
    outer_held = links.step_b(outer_sent)
    back = front_back_call(
        core, lengths, query_low, key_low, value_low, context_grad, first, hat_embed, inv_embed,
        embed_scale, matrices,
    )
    back, inner_across, outer_held = tie(back, inner_across, outer_held)
    (
        query_low_grad, key_low_grad, value_low_grad, query_bias_gradient, value_bias_gradient,
        embedded_grad, embed_gain_gradient, embed_bias_gradient,
    ) = back
    own_left = jnp.where(core == 0, normed_low, context)
    sent_left = jnp.where(core == 0, context, normed_low)
    square_sent = [
        local_terms(normed_low, jnp.where(core == 0, value_low_grad, query_low_grad)),
        local_terms(sent_left, jnp.where(core == 0, attended_grad, key_low_grad)),
    ]
    square_own = [
        local_terms(normed_low, jnp.where(core == 0, query_low_grad, value_low_grad)),
        local_terms(own_left, jnp.where(core == 0, key_low_grad, attended_grad)),
    ]
    square_cross = [links.swap(item, 1) for item in square_sent]
    outer_half = add(outer_held, outer_kept)
    outer_across = links.swap(outer_half[:, rows:], 2)
    inner_half = links.fold_b(links.split(add(inner_near, inner_across), 0), 0)
    wide = width // 2
    leaving = jnp.einsum("ts,td->sd", route, embedded_grad, preferred_element_type=jnp.float32)
    leaving = leaving.astype(jnp.bfloat16).reshape(owners, cap, width)
    parts = 2
    cut = cap // parts
    known = jnp.stack(
        [
            item.reshape(owners, parts, cut).transpose(1, 0, 2)
            for item in (held_ids, links.swap(held_ids, 1))
        ],
        axis=1,
    ).reshape(-1)
    known_sets = [known]
    bit = 2
    while bit < groups:
        known_sets += [links.swap(item, bit) for item in known_sets]
        bit *= 2
    sums = [
        embed_gain_gradient, embed_bias_gradient, query_bias_gradient, value_bias_gradient,
        output_bias_gradient, middle_gain_gradient, middle_bias_gradient, outer_bias_gradient,
        final_gain_gradient, final_bias_gradient,
    ]
    inner_bias_gradient = jnp.stack(inner_bias_gradient)[jnp.stack(blocks)]
    vector_terms = jnp.concatenate(
        [item.reshape(1, width) for item in sums] + [inner_bias_gradient]
    )
    vector_terms = vector_terms.reshape(14, owners, rows).transpose(1, 0, 2)
    vector_terms = jnp.pad(vector_terms, ((0, 0), (0, 2), (0, width - rows)))
    vector_terms = vector_terms.reshape(owners, 2, 8, width).astype(jnp.bfloat16)
    place_terms = embedded_grad.reshape(owners, 2, place_part, width)
    late_terms = jnp.concatenate([place_terms, vector_terms], axis=2)
    late_cross = links.swap(pick(late_terms, 1 - core, 1), 1)
    bits = []
    bit = 2
    while bit < groups:
        bits.append(bit)
        bit *= 2

    def exchange(part):
        piece = leaving[:, part * cut : (part + 1) * cut]
        return lax.all_to_all(piece, "vocab", 0, 0, tiled=True)

    def beyond(landed):
        landed = landed.reshape(-1, width)
        mine, theirs = ordered(landed[:, :wide], landed[:, wide:])
        items = [jnp.concatenate([mine, links.swap(theirs, 1)])]
        for bit in bits:
            items = items + [links.swap(item, bit) for item in items]
        return items

    def table_term(pieces, known):
        return matmul((table_ids[:, None] == known[None, :]).astype(jnp.bfloat16), pieces)

    table_ids = lax.iota(jnp.int32, table_rows)
    late_whole = jnp.concatenate(
        [add(square_own[0], square_cross[0]), add(pick(late_terms, core, 1), late_cross)], axis=1
    )
    chip, second_part = dp // 2 % 2, rows // 2
    second_cut = add(square_own[1], square_cross[1]).reshape(owners, 2, second_part, width)
    second_kept, second_sent = pick(second_cut, chip, 1), pick(second_cut, 1 - chip, 1)
    landed, late_whole, leaving, outer_across, inner_half, second_kept, second_sent = tie(
        exchange(0), links.split(late_whole, 0), leaving, outer_across, inner_half, second_kept,
        second_sent,
    )
    second_across = links.swap(second_sent, 2)
    late_sent, late_kept = links.last_b(late_whole, 0)
    late_held = links.step_b(late_sent)
    first_sets = beyond(landed)
    outer_cut = links.cut_a(add(outer_half[:, :rows], outer_across), 0)
    outer_arrived = links.sent_a(outer_cut)
    landed, first_sets, outer_arrived, second_across = tie(
        exchange(1), first_sets, outer_arrived, second_across
    )
    second_cut = links.split(add(second_kept, second_across), 0)
    second_sent, second_kept = links.last_b(second_cut, 0)
    second_held = links.step_b(second_sent)
    inner_cut = links.cut_a(inner_half, 0)
    inner_arrived = links.sent_a(inner_cut)
    second_sets = beyond(landed)
    table_sum = [table_term(jnp.concatenate([first_sets[0], second_sets[0]]), known_sets[0])]
    table_sum, late_held, second_held, second_sets, inner_arrived = tie(
        table_sum, late_held, second_held, second_sets, inner_arrived
    )
    late_half = jnp.concatenate([add(late_held, late_kept), add(second_held, second_kept)], axis=1)
    late_cut = links.cut_a(late_half, 0)
    late_arrived = links.sent_a(late_cut)
    hidden_share = jnp.concatenate(
        [add(outer_cut[0], *outer_arrived), add(inner_cut[0], *inner_arrived)]
    )
    hidden_share = links.far(hidden_share, 4)
    hidden_beyond = links.swap(hidden_share, 2)
    for i in range(1, len(known_sets)):
        pieces = jnp.concatenate([first_sets[i], second_sets[i]])
        table_sum.append(table_term(pieces, known_sets[i]))
    while len(table_sum) > 1:
        table_sum = [a + b for a, b in zip(table_sum[::2], table_sum[1::2])]
    table_half, hidden_beyond, late_arrived = tie(
        table_sum[0].astype(jnp.bfloat16), hidden_beyond, late_arrived
    )
    late_share = add(late_cut[0], *late_arrived)
    hidden_core = jnp.stack([hidden_share, hidden_beyond])
    hidden_other = links.swap(hidden_core, 1)
    table_other = links.swap(table_half, 1)
    late_main = links.far(late_share[: late_share.shape[0] - second_part], 2)
    late_second = links.far(late_share[late_share.shape[0] - second_part :], 4)
    late_core = jnp.concatenate([late_main, late_second, links.swap(late_second, 2)])
    hidden_gradients = finish_hidden_call(quarter, hidden_core, hidden_other)
    late_core, hidden_gradients = tie(late_core, hidden_gradients)
    outer_weight_gradient, inner_weight_gradient = hidden_gradients
    table_gradient = widen_call(core, table_half, table_other)
    late_other, table_gradient = tie(links.swap(late_core, 1), table_gradient)
    first_share, second_share, third_share, fourth_share, position_gradient, vector_share = (
        finish_late_call(core, chip, late_core, late_other, rows, place_part)
    )
    vector_share = vector_share[:, :rows]
    (
        embed_gain_gradient, embed_bias_gradient, query_bias_gradient, value_bias_gradient,
        output_bias_gradient, middle_gain_gradient, middle_bias_gradient, outer_bias_gradient,
        final_gain_gradient, final_bias_gradient,
    ) = (vector_share[i] for i in range(10))
    inner_bias_gradient = vector_share[10:14].reshape(4 * rows)

    return (
        output,
        table_gradient,
        position_gradient,
        embed_gain_gradient,
        embed_bias_gradient,
        first_share,
        query_bias_gradient,
        second_share,
        third_share,
        value_bias_gradient,
        fourth_share,
        output_bias_gradient,
        middle_gain_gradient,
        middle_bias_gradient,
        inner_weight_gradient,
        inner_bias_gradient,
        outer_weight_gradient,
        outer_bias_gradient,
        final_gain_gradient,
        final_bias_gradient,
    )


def solution(mesh):
    return jax.shard_map(
        functools.partial(on_device, mesh.shape["dp"], mesh.shape["vocab"]),
        mesh=mesh,
        in_specs=(
            P(("dp", "vocab"), None),
            P(("dp", "vocab")),
            P("vocab", None),
            P("vocab", None),
            P("vocab"),
            P("vocab"),
            P("vocab", None),
            P("vocab"),
            P("vocab", None),
            P("vocab", None),
            P("vocab"),
            P("vocab", None),
            P("vocab"),
            P("vocab"),
            P("vocab"),
            P("vocab", None),
            P("vocab"),
            P("vocab", None),
            P("vocab"),
            P("vocab"),
            P("vocab"),
            P(("dp", "vocab"), None, None),
        ),
        out_specs=(
            P(("dp", "vocab"), None, None),
            P("vocab", None),
            P("vocab", None),
            P("vocab"),
            P("vocab"),
            P("vocab", None),
            P("vocab"),
            P("vocab", None),
            P("vocab", None),
            P("vocab"),
            P("vocab", None),
            P("vocab"),
            P("vocab"),
            P("vocab"),
            P("vocab", None),
            P("vocab"),
            P("vocab", None),
            P("vocab"),
            P("vocab"),
            P("vocab"),
        ),
        check_vma=False,
    )
```
